1024 devices in a mesh: gx: 16 (over x, core), gy: 64 (over z, y).
Axes of the slice: x: 8, y: 8, z: 8, core: 2. Of those that a mesh axis runs over, the one named last changes fastest.
Arguments:
- stream_vel: float32 [512, 16, 2048], P('gy', None, 'gx'), may hold values from -6 to 6
- normal_vel: float32 [512, 16, 2048], P('gy', None, 'gx'), may hold values from -6 to 6
- span_vel: float32 [512, 16, 2048], P('gy', None, 'gx'), may hold values from -6 to 6
Outputs:
- pressure: float32 [512, 16, 2048], P('gy', None, 'gx')
- stream_next: float32 [512, 16, 2048], P('gy', None, 'gx')
- normal_next: float32 [512, 16, 2048], P('gy', None, 'gx')
- span_next: float32 [512, 16, 2048], P('gy', None, 'gx')
The draws below stay inside these ranges and needn't reach their ends.
All inputs are finite; a program needn't handle non-finite values.
Results may differ from the reference program's by a relative error of at most 0.0004.
Values sent between devices are 32-bit elements; how exact they have to be, the bound alone decides.
No kernel may reach another device: no remote copies, remote signals or barrier semaphores. Data moves between devices by JAX's collectives and lax.ppermute only.
A program may use at most 32 MiB of HBM per device.

```python
import math
import jax
import jax.numpy as jnp
from jax import lax

NZ = 16
NX = 2048
NY = 512


def levels(key, dims, cuts, smallest, largest):
    def one(position, parts):
        steps = jax.random.uniform(jax.random.fold_in(jax.random.fold_in(key, 6), position), (parts,), jnp.float32, smallest / len(cuts), largest / len(cuts))
        return jnp.repeat(jnp.exp(steps), dims[position] // parts).reshape((-1,) + (1,) * (len(dims) - position - 1))

    gain = one(*cuts[0])
    for cut in cuts[1:]:
        gain = gain * one(*cut)
    return gain


def noise(rng, dims, width, limit, shards=(), kind=jnp.bfloat16):
    loudness = levels(rng, dims, shards, -0.22, 0.18) if shards else 1.0
    array = jax.random.normal(rng, dims, jnp.float32) * width * loudness
    return jnp.minimum(jnp.maximum(array, -limit), limit).astype(kind)


def setup_inputs(seed: int = 0) -> dict:
    keys = jax.random.split(jax.random.key(seed), 4)
    stream_vel = noise(keys[0], (NY, NZ, NX), 1.0, 6.0, ((0, 64), (2, 16)), jnp.float32)
    normal_vel = noise(keys[1], (NY, NZ, NX), 1.0, 6.0, ((0, 64), (2, 16)), jnp.float32)
    span_vel = noise(keys[2], (NY, NZ, NX), 1.0, 6.0, ((0, 64), (2, 16)), jnp.float32)
    return dict(stream_vel=stream_vel, normal_vel=normal_vel, span_vel=span_vel)


shift_term = 1.0 / 1024.0
grid_ratio = 1.0 / 128.0

def reference(stream_vel, normal_vel, span_vel):
    count_y, count_z, count_x = stream_vel.shape
    float_type = stream_vel.dtype
    row_index = jnp.arange(count_y)
    wall_keep = (row_index < count_y - 1).astype(float_type)[:, None, None]
    normal_wall = normal_vel * wall_keep
    normal_below = jnp.concatenate([jnp.zeros_like(normal_wall[:1]), normal_wall[:-1]], axis=0)
    source = grid_ratio * (stream_vel - jnp.roll(stream_vel, 1, axis=2)) + (normal_wall - normal_below) + grid_ratio * (span_vel - jnp.roll(span_vel, 1, axis=1))
    spectrum = jnp.fft.fft(jnp.fft.fft(source, axis=1), axis=2)
    wave_z = (2.0 * jnp.sin(math.pi * jnp.arange(count_z).astype(float_type) / count_z)) ** 2
    wave_x = (2.0 * jnp.sin(math.pi * jnp.arange(count_x).astype(float_type) / count_x)) ** 2
    eigen_sum = grid_ratio * grid_ratio * (wave_z[:, None] + wave_x[None, :]) + shift_term
    lower_band = jnp.broadcast_to((row_index > 0).astype(float_type)[None, :], (count_x, count_y))
    upper_band = jnp.broadcast_to((row_index < count_y - 1).astype(float_type)[None, :], (count_x, count_y))
    end_extra = (row_index == 0).astype(float_type) + (row_index == count_y - 1).astype(float_type)

    def solve_plane(plane_inputs):
        plane, eigen_row = plane_inputs
        diagonal = -(2.0 + eigen_row)[:, None] + end_extra[None, :]
        right_side = jnp.stack([jnp.real(plane).T, jnp.imag(plane).T], axis=-1)
        solved = lax.linalg.tridiagonal_solve(lower_band, diagonal, upper_band, right_side)
        return (solved[..., 0].T, solved[..., 1].T)
    solved_re, solved_im = lax.map(solve_plane, (jnp.moveaxis(spectrum, 1, 0), eigen_sum))
    pressure_hat = lax.complex(jnp.moveaxis(solved_re, 0, 1), jnp.moveaxis(solved_im, 0, 1))
    pressure = jnp.real(jnp.fft.ifft(jnp.fft.ifft(pressure_hat, axis=2), axis=1)).astype(float_type)
    pressure_up = jnp.concatenate([pressure[1:], jnp.zeros_like(pressure[:1])], axis=0)
    stream_next = stream_vel - grid_ratio * (jnp.roll(pressure, -1, axis=2) - pressure)
    normal_next = (normal_vel - (pressure_up - pressure)) * wall_keep
    span_next = span_vel - grid_ratio * (jnp.roll(pressure, -1, axis=1) - pressure)
    return (pressure, stream_next, normal_next, span_next)
```

```python
import functools
import math

import jax
import jax.numpy as jnp
import numpy as np
from jax import lax
from jax.experimental import pallas as pl
from jax.experimental.pallas import tpu as pltpu
from jax.sharding import PartitionSpec as P

shift_term = 1.0 / 1024.0
grid_ratio = 1.0 / 128.0
highest = lax.Precision.HIGHEST


def weighted(terms):
    total = None
    for factor, value in terms:
        if abs(factor) < 1e-12:
            continue
        term = value * factor
        total = term if total is None else total + term
    return total


def angle_tables(count):
    half = count // 2
    cosine = [[math.cos(2 * math.pi * (k * i % count) / count) for i in range(count)] for k in range(half + 1)]
    sine = [[math.sin(2 * math.pi * (k * i % count) / count) for i in range(count)] for k in range(half + 1)]
    return cosine, sine


def real_forward(values):
    count = len(values)
    half = count // 2
    cosine, sine = angle_tables(count)
    even = [values[0]] + [values[i] + values[count - i] for i in range(1, half)] + [values[half]]
    odd = [None] + [values[i] - values[count - i] for i in range(1, half)]
    edge, inner = 1 / math.sqrt(count), math.sqrt(2 / count)
    first = weighted([(edge, value) for value in even])
    middle = weighted([(edge * (-1) ** i, value) for i, value in enumerate(even)])
    cosines = [weighted([(inner * cosine[k][i], even[i]) for i in range(half + 1)]) for k in range(1, half)]
    sines = [weighted([(-inner * sine[k][i], odd[i]) for i in range(1, half)]) for k in range(1, half)]
    return [first, middle, *cosines, *sines]


def real_inverse(planes):
    count = len(planes)
    half = count // 2
    cosine, sine = angle_tables(count)
    edge, inner = 1 / math.sqrt(count), math.sqrt(2 / count)
    values = [None] * count
    for i in range(half + 1):
        even = weighted(
            [(edge, planes[0]), (edge * (-1) ** i, planes[1])]
            + [(inner * cosine[k][i], planes[k + 1]) for k in range(1, half)]
        )
        if i in (0, half):
            values[i] = even
            continue
        odd = weighted([(-inner * sine[k][i], planes[half + k]) for k in range(1, half)])
        values[i] = even + odd
        values[count - i] = even - odd
    return values


def plane_modes(count):
    half = count // 2
    return np.array([0, half, *range(1, half), *range(1, half)])


def tables(planes, lanes, blocks, length_x):
    half = blocks // 2
    t = np.arange(lanes)
    phases = np.arange(half)
    turn = 2 * np.pi * phases[:, None] * t[None, :] / length_x
    turns = np.concatenate([np.cos(turn), np.sin(turn)])
    product = 2 * np.pi * (t[:, None] * t[None, :] % lanes) / lanes
    scale = 1 / math.sqrt(lanes)
    c, s = np.cos(product) * scale, np.sin(product) * scale
    inner = np.block([[c, -s], [s, c]])
    root = math.sqrt(2.0)
    n = lanes // 2
    first = np.concatenate([c[:, :1], root * c[:, 1:n], c[:, n : n + 1], -root * s[:, 1:n]], axis=1)
    shifted = np.pi * (t[:, None] * (2 * np.arange(n)[None, :] + 1) % (2 * lanes)) / lanes
    middle = root * scale * np.concatenate([np.cos(shifted), -np.sin(shifted)], axis=1)
    zero = np.zeros((lanes, lanes))
    outer = np.block([[first, zero], [zero, middle]])
    mode_x = np.zeros((half, 2 * lanes))
    mode_x[1:] = phases[1:, None] + blocks * np.concatenate([t, t])[None, :]
    mode_x[0, : n + 1] = blocks * np.arange(n + 1)
    mode_x[0, n + 1 : lanes] = blocks * np.arange(1, n)
    mode_x[0, lanes:] = half + blocks * np.concatenate([np.arange(n), np.arange(n)])
    wave_x = (2 * np.sin(np.pi * mode_x / length_x)) ** 2
    wave_z = (2 * np.sin(np.pi * plane_modes(planes) / planes)) ** 2
    eigen_sum = grid_ratio * grid_ratio * (wave_z[:, None, None] + wave_x[None]) + shift_term
    decay = 2 * np.arcsinh(np.sqrt(eigen_sum) / 2)
    decay = decay.reshape(planes * half, 2 * lanes)
    return tuple(jnp.asarray(a, jnp.float32) for a in (turns, inner, outer, decay))


def places(shape):
    return lax.broadcasted_iota(jnp.int32, shape, 0), lax.broadcasted_iota(jnp.int32, shape, 1)


def column_to_row(column, row, lane):
    return jnp.sum(jnp.where(row == lane, column, 0.0), axis=0, keepdims=True)


def row_to_column(line, row, lane):
    return jnp.sum(jnp.where(row == lane, line, 0.0), axis=1, keepdims=True)


def wall_keep(row, last_row, parts_y):
    is_wall = jnp.logical_and(row == last_row, lax.axis_index("gy") == parts_y - 1)
    return jnp.where(is_wall, 0.0, 1.0)


def source_kernel(planes, parts_y, stream_ref, normal_ref, span_ref, out_ref):
    cells = stream_ref.shape[1]
    rows = stream_ref.shape[0] // planes
    row, lane = places((rows, cells))
    keep = wall_keep(row, rows - 1, parts_y)

    def plane(ref, z):
        return ref[pl.ds(z, rows, stride=planes), :]

    main, rim = [], []
    span_before = plane(span_ref, planes - 1)
    for z in range(planes):
        stream, normal, span = plane(stream_ref, z), plane(normal_ref, z) * keep, plane(span_ref, z)
        stream_left = jnp.where(lane == 0, 0.0, pltpu.roll(stream, 1, 1))
        normal_turned = pltpu.roll(normal, 1, 0)
        normal_below = jnp.where(row == 0, 0.0, normal_turned)
        main.append(
            grid_ratio * (stream - stream_left) + (normal - normal_below) + grid_ratio * (span - span_before)
        )
        ends = column_to_row(stream[:, cells - 1 :], row, lane)
        rim.append(jnp.where(row == 0, -normal_turned, jnp.where(row == 1, -grid_ratio * ends, 0.0)))
        span_before = span
    main, rim = real_forward(main), real_forward(rim)
    for k in range(planes):
        out_ref[k, :rows, :] = main[k]
        out_ref[k, rows:, :] = rim[k]


class Line:
    def __init__(self, decay, rows, parts_y):
        base = (lax.axis_index("gy") * rows).astype(jnp.float32)
        total = rows * parts_y
        self.step = jnp.exp(-decay)
        square, grown = self.step * self.step, jnp.exp(2.0 * decay)
        low = jnp.exp(-decay * (2.0 * base + 1.0))
        high = jnp.exp(-decay * (2.0 * (total - base) - 1.0))
        self.low, self.high = [], []
        for _ in range(rows + 1):
            self.low.append(1.0 + low)
            self.high.append(1.0 + high)
            low, high = low * square, high * grown
        self.decay, self.total = decay, total

    def gain(self):
        return -1.0 / ((jnp.exp(self.decay) - self.step) * (1.0 - jnp.exp(self.decay * (-2.0 * self.total))))


def decay_here(decay_ref, half):
    start = pl.multiple_of(lax.axis_index("gx") * half, half)
    return decay_ref[pl.ds(start, half), :]


def modes_kernel(rows, parts_y, in_ref, turns_ref, inner_ref, outer_ref, decay_ref, send_ref, modes_ref, left, edge):
    blocks, _, lanes = in_ref.shape
    half = blocks // 2
    row, lane = places((rows, lanes))
    main = [in_ref[d, :rows, :] for d in range(blocks)]
    rim = [in_ref[d, rows:, :] for d in range(blocks)]
    for d in range(blocks):
        ends = row_to_column(rim[d - 1][1:2, :], row, lane)
        main[d] = main[d] + jnp.where(lane == 0, ends, 0.0)
    main = real_forward(main)
    rim = real_forward([piece[:1, :] for piece in rim])
    edge[...] = jnp.zeros_like(edge)
    for h in range(2):
        edge[:rows, h * lanes : (h + 1) * lanes] = main[h]
        edge[rows : rows + 1, h * lanes : (h + 1) * lanes] = rim[h]
        left[h, pl.ds(0, rows, stride=half), :] = main[h]
        left[h, rows * half : rows * half + 1, :] = rim[h]
    for a in range(1, half):
        c, s = turns_ref[a : a + 1, :], turns_ref[half + a : half + a + 1, :]
        for first, count, (re, im) in (
            (a, rows, (main[a + 1], main[half + a])),
            (rows * half + a, 1, (rim[a + 1], rim[half + a])),
        ):
            left[0, pl.ds(first, count, stride=half), :] = re * c + im * s
            left[1, pl.ds(first, count, stride=half), :] = im * c - re * s
    inner = jnp.dot(
        jnp.concatenate([left[0], left[1]], axis=1), inner_ref[...], precision=highest, preferred_element_type=jnp.float32
    )
    outer = jnp.dot(edge[...], outer_ref[...], precision=highest, preferred_element_type=jnp.float32)
    for h in range(2):
        part = slice(h * lanes, (h + 1) * lanes)
        modes_ref[h, :, :] = inner[:, part]
        modes_ref[h, pl.ds(0, rows, stride=half), :] = outer[:rows, part]
        modes_ref[h, rows * half : rows * half + 1, :] = outer[rows : rows + 1, part]
    spectrum = row_list(modes_ref, rows, half)
    line = Line(decay_here(decay_ref, half), rows, parts_y)
    below = line.low[0] * spectrum[0]
    above = line.high[rows] * spectrum[rows]
    for i in range(1, rows + 1):
        below = line.low[i] * spectrum[i] + line.step * below
        above = line.high[rows - i] * spectrum[rows - i] + line.step * above
    for copy in range(send_ref.shape[0]):
        send_ref[copy, :half, :] = below
        send_ref[copy, half:, :] = above


def row_list(modes_ref, rows, half):
    return [
        jnp.concatenate([modes_ref[h, i * half : (i + 1) * half, :] for h in range(2)], axis=1)
        for i in range(rows + 1)
    ]


def running(pieces, mine, step, half):
    count = pieces.shape[0]
    below = above = jnp.zeros_like(step)
    below_mine = above_mine = below
    for i in range(count):
        below_mine = jnp.where(mine == i, below, below_mine)
        above_mine = jnp.where(mine == count - 1 - i, above, above_mine)
        below = pieces[i, :half, :] + step * below
        above = pieces[count - 1 - i, half:, :] + step * above
    return below_mine, above_mine, below, above


def near_kernel(rows, near, in_ref, decay_ref, mine_ref, send_ref):
    half = in_ref.shape[1] // 2
    decay = decay_here(decay_ref, half)
    place = lax.rem(lax.axis_index("gy"), near)
    below_mine, above_mine, below, above = running(in_ref, place, jnp.exp(-rows * decay), half)
    mine_ref[:half, :] = below_mine
    mine_ref[half:, :] = above_mine
    for copy in range(send_ref.shape[0]):
        send_ref[copy, :half, :] = below
        send_ref[copy, half:, :] = above


def solve_kernel(
    rows, parts_y, near, in_ref, mine_ref, modes_ref, turns_ref, inner_ref, outer_ref, decay_ref, out_ref, left, edge
):
    blocks, _, lanes = out_ref.shape
    half = blocks // 2
    row, lane = places((rows, lanes))
    decay = decay_here(decay_ref, half)
    place, far_place = lax.rem(lax.axis_index("gy"), near), lax.div(lax.axis_index("gy"), near)
    far_below, far_above, _, _ = running(in_ref, far_place, jnp.exp(-(rows * near) * decay), half)
    ahead = (rows * place).astype(jnp.float32)
    below = mine_ref[:half, :] + jnp.exp(-decay * ahead) * far_below
    above = mine_ref[half:, :] + jnp.exp(-decay * (rows * (near - 1) - ahead)) * far_above
    line = Line(decay, rows, parts_y)
    spectrum = row_list(modes_ref, rows, half)
    gain = line.gain()
    from_below = [line.low[0] * spectrum[0] + below]
    for i in range(1, rows + 1):
        from_below.append(line.low[i] * spectrum[i] + line.step * from_below[-1])
    from_above = above
    edge[...] = jnp.zeros_like(edge)
    for i in reversed(range(rows + 1)):
        solved = gain * (line.high[i] * from_below[i] + line.low[i] * from_above)
        edge[i : i + 1, :] = solved[:1, :]
        for h in range(2):
            left[h, i * half : (i + 1) * half, :] = solved[:, h * lanes : (h + 1) * lanes]
        from_above = line.step * (from_above + line.high[i] * spectrum[i])
    back = (((1,), (1,)), ((), ()))
    inner = lax.dot_general(
        jnp.concatenate([left[0], left[1]], axis=1),
        inner_ref[...],
        back,
        precision=highest,
        preferred_element_type=jnp.float32,
    )
    outer = lax.dot_general(
        edge[...], outer_ref[...], back, precision=highest, preferred_element_type=jnp.float32
    )
    for h in range(2):
        left[h, :, :] = inner[:, h * lanes : (h + 1) * lanes]
    main = [outer[:rows, :lanes], outer[:rows, lanes:]] + [None] * (blocks - 2)
    rim = [outer[rows : rows + 1, :lanes], outer[rows : rows + 1, lanes:]] + [None] * (blocks - 2)
    for a in range(1, half):
        c, s = turns_ref[a : a + 1, :], turns_ref[half + a : half + a + 1, :]
        for planes, first, count in ((main, a, rows), (rim, rows * half + a, 1)):
            re = left[0, pl.ds(first, count, stride=half), :]
            im = left[1, pl.ds(first, count, stride=half), :]
            planes[a + 1] = re * c - im * s
            planes[half + a] = im * c + re * s
    main, rim = real_inverse(main), real_inverse(rim)
    for d in range(blocks):
        out_ref[d, :rows, :] = main[d]
        ends = column_to_row(main[(d + 1) % blocks][:, :1], row, lane)
        out_ref[d, rows:, :] = jnp.where(row == 0, rim[d], jnp.where(row == 1, ends, 0.0))


def correct_kernel(
    parts_y, in_ref, stream_ref, normal_ref, span_ref, pressure_ref, stream_out, normal_out, span_out
):
    planes, _, cells = in_ref.shape
    rows = stream_ref.shape[0] // planes
    row, lane = places((rows, cells))
    keep = wall_keep(row, rows - 1, parts_y)
    pressure = real_inverse([in_ref[k, :rows, :] for k in range(planes)])
    rim = real_inverse([in_ref[k, rows:, :] for k in range(planes)])
    for z in range(planes):
        here = pl.ds(z, rows, stride=planes)
        p = pressure[z]
        upper = jnp.where(row == rows - 1, rim[z][:1, :], pltpu.roll(p, rows - 1, 0))
        right = jnp.where(lane == cells - 1, row_to_column(rim[z][1:2, :], row, lane), pltpu.roll(p, cells - 1, 1))
        pressure_ref[here, :] = p
        stream_out[here, :] = stream_ref[here, :] - grid_ratio * (right - p)
        normal_out[here, :] = (normal_ref[here, :] - (upper - p)) * keep
        span_out[here, :] = span_ref[here, :] - grid_ratio * (pressure[(z + 1) % planes] - p)


def shape_of(*dims):
    return jax.ShapeDtypeStruct(dims, jnp.float32)


def per_device(stream_vel, normal_vel, span_vel):
    rows, planes, cells = stream_vel.shape
    parts_x, parts_y = lax.axis_size("gx"), lax.axis_size("gy")
    blocks, half = parts_x, parts_x // 2
    near = 1 << (parts_y.bit_length() // 2)
    far = parts_y // near
    if planes != parts_x or rows != half or near * far != parts_y:
        raise ValueError("unsupported sizes")
    turns, inner, outer, decay = tables(planes, cells, blocks, cells * parts_x)
    near_groups = [[i * near + k for k in range(near)] for i in range(far)]
    far_groups = [[i + k * near for k in range(far)] for i in range(near)]
    flat = [a.reshape(rows * planes, cells) for a in (stream_vel, normal_vel, span_vel)]
    scratch = [pltpu.VMEM((2, (rows + 1) * half, cells), jnp.float32), pltpu.VMEM((2 * rows, 2 * cells), jnp.float32)]

    sent = pl.pallas_call(
        functools.partial(source_kernel, planes, parts_y), out_shape=shape_of(planes, 2 * rows, cells), name="source"
    )(*flat)
    taken = lax.all_to_all(sent, "gx", 0, 0)
    sent, modes = pl.pallas_call(
        functools.partial(modes_kernel, rows, parts_y),
        out_shape=(shape_of(near, 2 * half, 2 * cells), shape_of(2, (rows + 1) * half, cells)),
        scratch_shapes=scratch,
        name="modes",
    )(taken, turns, inner, outer, decay)
    taken = lax.all_to_all(sent, "gy", 0, 0, axis_index_groups=near_groups)
    mine, sent = pl.pallas_call(
        functools.partial(near_kernel, rows, near),
        out_shape=(shape_of(2 * half, 2 * cells), shape_of(far, 2 * half, 2 * cells)),
        name="near",
    )(taken, decay)
    taken = lax.all_to_all(sent, "gy", 0, 0, axis_index_groups=far_groups)
    sent = pl.pallas_call(
        functools.partial(solve_kernel, rows, parts_y, near),
        out_shape=shape_of(blocks, 2 * rows, cells),
        scratch_shapes=scratch,
        name="solve",
    )(taken, mine, modes, turns, inner, outer, decay)
    taken = lax.all_to_all(sent, "gx", 0, 0)
    outs = pl.pallas_call(
        functools.partial(correct_kernel, parts_y), out_shape=(shape_of(rows * planes, cells),) * 4, name="correct"
    )(taken, *flat)
    return tuple(a.reshape(rows, planes, cells) for a in outs)


def solution(mesh):
    spec = P("gy", None, "gx")
    return jax.shard_map(
        per_device, mesh=mesh, in_specs=(spec,) * 3, out_specs=(spec,) * 4, check_vma=False
    )
```

```python
import functools
import math

import jax
import jax.numpy as jnp
import numpy as np
from jax import lax
from jax.experimental import pallas as pl
from jax.experimental.pallas import tpu as pltpu
from jax.sharding import PartitionSpec as P

shift_term = 1.0 / 1024.0
grid_ratio = 1.0 / 128.0
highest = lax.Precision.HIGHEST


def weighted(terms):
    total = None
    for factor, value in terms:
        if abs(factor) < 1e-12:
            continue
        term = value * factor
        total = term if total is None else total + term
    return total


def angle_tables(count):
    half = count // 2
    cosine = [[math.cos(2 * math.pi * (k * i % count) / count) for i in range(count)] for k in range(half + 1)]
    sine = [[math.sin(2 * math.pi * (k * i % count) / count) for i in range(count)] for k in range(half + 1)]
    return cosine, sine


def real_forward(values):
    count = len(values)
    half = count // 2
    cosine, sine = angle_tables(count)
    even = [values[0]] + [values[i] + values[count - i] for i in range(1, half)] + [values[half]]
    odd = [None] + [values[i] - values[count - i] for i in range(1, half)]
    edge, inner = 1 / math.sqrt(count), math.sqrt(2 / count)
    first = weighted([(edge, value) for value in even])
    middle = weighted([(edge * (-1) ** i, value) for i, value in enumerate(even)])
    cosines = [weighted([(inner * cosine[k][i], even[i]) for i in range(half + 1)]) for k in range(1, half)]
    sines = [weighted([(-inner * sine[k][i], odd[i]) for i in range(1, half)]) for k in range(1, half)]
    return [first, middle, *cosines, *sines]


def real_inverse(planes):
    count = len(planes)
    half = count // 2
    cosine, sine = angle_tables(count)
    edge, inner = 1 / math.sqrt(count), math.sqrt(2 / count)
    values = [None] * count
    for i in range(half + 1):
        even = weighted(
            [(edge, planes[0]), (edge * (-1) ** i, planes[1])]
            + [(inner * cosine[k][i], planes[k + 1]) for k in range(1, half)]
        )
        if i in (0, half):
            values[i] = even
            continue
        odd = weighted([(-inner * sine[k][i], planes[half + k]) for k in range(1, half)])
        values[i] = even + odd
        values[count - i] = even - odd
    return values


def plane_modes(count):
    half = count // 2
    return np.array([0, half, *range(1, half), *range(1, half)])


def tables(planes, lanes, blocks, length_x):
    half = blocks // 2
    t = np.arange(lanes)
    phases = np.arange(half)
    turn = 2 * np.pi * phases[:, None] * t[None, :] / length_x
    turns = np.concatenate([np.cos(turn), np.sin(turn)])
    product = 2 * np.pi * (t[:, None] * t[None, :] % lanes) / lanes
    scale = 1 / math.sqrt(lanes)
    c, s = np.cos(product) * scale, np.sin(product) * scale
    inner = np.block([[c, -s], [s, c]])
    root = math.sqrt(2.0)
    n = lanes // 2
    first = np.concatenate([c[:, :1], root * c[:, 1:n], c[:, n : n + 1], -root * s[:, 1:n]], axis=1)
    shifted = np.pi * (t[:, None] * (2 * np.arange(n)[None, :] + 1) % (2 * lanes)) / lanes
    middle = root * scale * np.concatenate([np.cos(shifted), -np.sin(shifted)], axis=1)
    zero = np.zeros((lanes, lanes))
    outer = np.block([[first, zero], [zero, middle]])
    mode_x = np.zeros((half, 2 * lanes))
    mode_x[1:] = phases[1:, None] + blocks * np.concatenate([t, t])[None, :]
    mode_x[0, : n + 1] = blocks * np.arange(n + 1)
    mode_x[0, n + 1 : lanes] = blocks * np.arange(1, n)
    mode_x[0, lanes:] = half + blocks * np.concatenate([np.arange(n), np.arange(n)])
    wave_x = (2 * np.sin(np.pi * mode_x / length_x)) ** 2
    wave_z = (2 * np.sin(np.pi * plane_modes(planes) / planes)) ** 2
    eigen_sum = grid_ratio * grid_ratio * (wave_z[:, None, None] + wave_x[None]) + shift_term
    decay = 2 * np.arcsinh(np.sqrt(eigen_sum) / 2)
    decay = decay.reshape(planes * half, 2 * lanes)
    return tuple(jnp.asarray(a, jnp.float32) for a in (turns, inner, outer, decay))


def places(shape):
    return lax.broadcasted_iota(jnp.int32, shape, 0), lax.broadcasted_iota(jnp.int32, shape, 1)


def column_to_row(column, row, lane):
    return jnp.sum(jnp.where(row == lane, column, 0.0), axis=0, keepdims=True)


def row_to_column(line, row, lane):
    return jnp.sum(jnp.where(row == lane, line, 0.0), axis=1, keepdims=True)


def wall_keep(row, last_row, parts_y):
    is_wall = jnp.logical_and(row == last_row, lax.axis_index("gy") == parts_y - 1)
    return jnp.where(is_wall, 0.0, 1.0)


def source_kernel(planes, parts_y, stream_ref, normal_ref, span_ref, out_ref):
    cells = stream_ref.shape[1]
    rows = stream_ref.shape[0] // planes
    row, lane = places((rows, cells))
    keep = wall_keep(row, rows - 1, parts_y)

    def plane(ref, z):
        return ref[pl.ds(z, rows, stride=planes), :]

    main, rim = [], []
    span_before = plane(span_ref, planes - 1)
    for z in range(planes):
        stream, normal, span = plane(stream_ref, z), plane(normal_ref, z) * keep, plane(span_ref, z)
        stream_left = jnp.where(lane == 0, 0.0, pltpu.roll(stream, 1, 1))
        normal_turned = pltpu.roll(normal, 1, 0)
        normal_below = jnp.where(row == 0, 0.0, normal_turned)
        main.append(
            grid_ratio * (stream - stream_left) + (normal - normal_below) + grid_ratio * (span - span_before)
        )
        ends = column_to_row(stream[:, cells - 1 :], row, lane)
        rim.append(jnp.where(row == 0, -normal_turned, jnp.where(row == 1, -grid_ratio * ends, 0.0)))
        span_before = span
    main, rim = real_forward(main), real_forward(rim)
    for k in range(planes):
        out_ref[k, :rows, :] = main[k]
        out_ref[k, rows:, :] = rim[k]


class Line:
    def __init__(self, decay, rows, parts_y):
        base = (lax.axis_index("gy") * rows).astype(jnp.float32)
        total = rows * parts_y
        self.step = jnp.exp(-decay)
        square, grown = self.step * self.step, jnp.exp(2.0 * decay)
        low = jnp.exp(-decay * (2.0 * base + 1.0))
        high = jnp.exp(-decay * (2.0 * (total - base) - 1.0))
        self.low, self.high = [], []
        for _ in range(rows + 1):
            self.low.append(1.0 + low)
            self.high.append(1.0 + high)
            low, high = low * square, high * grown
        self.decay, self.total = decay, total

    def gain(self):
        return -1.0 / ((jnp.exp(self.decay) - self.step) * (1.0 - jnp.exp(self.decay * (-2.0 * self.total))))


def decay_here(decay_ref, half):
    start = pl.multiple_of(lax.axis_index("gx") * half, half)
    return decay_ref[pl.ds(start, half), :]


def modes_kernel(rows, parts_y, in_ref, turns_ref, inner_ref, outer_ref, decay_ref, send_ref, modes_ref, left, edge):
    blocks, _, lanes = in_ref.shape
    half = blocks // 2
    row, lane = places((rows, lanes))
    main = [in_ref[d, :rows, :] for d in range(blocks)]
    rim = [in_ref[d, rows:, :] for d in range(blocks)]
    for d in range(blocks):
        ends = row_to_column(rim[d - 1][1:2, :], row, lane)
        main[d] = main[d] + jnp.where(lane == 0, ends, 0.0)
    main = real_forward(main)
    rim = real_forward([piece[:1, :] for piece in rim])
    edge[...] = jnp.zeros_like(edge)
    for h in range(2):
        edge[:rows, h * lanes : (h + 1) * lanes] = main[h]
        edge[rows : rows + 1, h * lanes : (h + 1) * lanes] = rim[h]
        left[h, pl.ds(0, rows, stride=half), :] = main[h]
        left[h, rows * half : rows * half + 1, :] = rim[h]
    for a in range(1, half):
        c, s = turns_ref[a : a + 1, :], turns_ref[half + a : half + a + 1, :]
        for first, count, (re, im) in (
            (a, rows, (main[a + 1], main[half + a])),
            (rows * half + a, 1, (rim[a + 1], rim[half + a])),
        ):
            left[0, pl.ds(first, count, stride=half), :] = re * c + im * s
            left[1, pl.ds(first, count, stride=half), :] = im * c - re * s
    inner = jnp.dot(
        jnp.concatenate([left[0], left[1]], axis=1), inner_ref[...], precision=highest, preferred_element_type=jnp.float32
    )
    outer = jnp.dot(edge[...], outer_ref[...], precision=highest, preferred_element_type=jnp.float32)
    for h in range(2):
        part = slice(h * lanes, (h + 1) * lanes)
        modes_ref[h, :, :] = inner[:, part]
        modes_ref[h, pl.ds(0, rows, stride=half), :] = outer[:rows, part]
        modes_ref[h, rows * half : rows * half + 1, :] = outer[rows : rows + 1, part]
    spectrum = row_list(modes_ref, rows, half)
    line = Line(decay_here(decay_ref, half), rows, parts_y)
    below = line.low[0] * spectrum[0]
    above = line.high[rows] * spectrum[rows]
    for i in range(1, rows + 1):
        below = line.low[i] * spectrum[i] + line.step * below
        above = line.high[rows - i] * spectrum[rows - i] + line.step * above
    mine = lax.axis_index("gy")
    for other in range(parts_y):
        send_ref[other, :, :] = jnp.where(mine < other, below, above)


def row_list(modes_ref, rows, half):
    return [
        jnp.concatenate([modes_ref[h, i * half : (i + 1) * half, :] for h in range(2)], axis=1)
        for i in range(rows + 1)
    ]


def entering(pieces_ref, mine, step, group):
    count = pieces_ref.shape[0]
    zero = jnp.zeros_like(step)
    below = above = zero
    for first in range(0, count, group):
        part = zero
        kept = jnp.ones_like(step)
        for i in range(first, min(first + group, count)):
            part = jnp.where(i < mine, pieces_ref[i] + step * part, part)
            kept = jnp.where(i < mine, step * kept, kept)
        below = part + kept * below
        part = zero
        kept = jnp.ones_like(step)
        for i in range(first, min(first + group, count)):
            j = count - 1 - i
            part = jnp.where(j > mine, pieces_ref[j] + step * part, part)
            kept = jnp.where(j > mine, step * kept, kept)
        above = part + kept * above
    return below, above


def solve_kernel(
    rows, parts_y, in_ref, modes_ref, turns_ref, inner_ref, outer_ref, decay_ref, out_ref, left, edge
):
    blocks, _, lanes = out_ref.shape
    half = blocks // 2
    row, lane = places((rows, lanes))
    decay = decay_here(decay_ref, half)
    below, above = entering(in_ref, lax.axis_index("gy"), jnp.exp(-rows * decay), 8)
    line = Line(decay, rows, parts_y)
    spectrum = row_list(modes_ref, rows, half)
    gain = line.gain()
    from_below = [line.low[0] * spectrum[0] + below]
    for i in range(1, rows + 1):
        from_below.append(line.low[i] * spectrum[i] + line.step * from_below[-1])
    from_above = above
    edge[...] = jnp.zeros_like(edge)
    for i in reversed(range(rows + 1)):
        solved = gain * (line.high[i] * from_below[i] + line.low[i] * from_above)
        edge[i : i + 1, :] = solved[:1, :]
        for h in range(2):
            left[h, i * half : (i + 1) * half, :] = solved[:, h * lanes : (h + 1) * lanes]
        from_above = line.step * (from_above + line.high[i] * spectrum[i])
    back = (((1,), (1,)), ((), ()))
    inner = lax.dot_general(
        jnp.concatenate([left[0], left[1]], axis=1),
        inner_ref[...],
        back,
        precision=highest,
        preferred_element_type=jnp.float32,
    )
    outer = lax.dot_general(
        edge[...], outer_ref[...], back, precision=highest, preferred_element_type=jnp.float32
    )
    for h in range(2):
        left[h, :, :] = inner[:, h * lanes : (h + 1) * lanes]
    main = [outer[:rows, :lanes], outer[:rows, lanes:]] + [None] * (blocks - 2)
    rim = [outer[rows : rows + 1, :lanes], outer[rows : rows + 1, lanes:]] + [None] * (blocks - 2)
    for a in range(1, half):
        c, s = turns_ref[a : a + 1, :], turns_ref[half + a : half + a + 1, :]
        for planes, first, count in ((main, a, rows), (rim, rows * half + a, 1)):
            re = left[0, pl.ds(first, count, stride=half), :]
            im = left[1, pl.ds(first, count, stride=half), :]
            planes[a + 1] = re * c - im * s
            planes[half + a] = im * c + re * s
    main, rim = real_inverse(main), real_inverse(rim)
    for d in range(blocks):
        out_ref[d, :rows, :] = main[d]
        ends = column_to_row(main[(d + 1) % blocks][:, :1], row, lane)
        out_ref[d, rows:, :] = jnp.where(row == 0, rim[d], jnp.where(row == 1, ends, 0.0))


def correct_kernel(
    parts_y, in_ref, stream_ref, normal_ref, span_ref, pressure_ref, stream_out, normal_out, span_out
):
    planes, _, cells = in_ref.shape
    rows = stream_ref.shape[0] // planes
    row, lane = places((rows, cells))
    keep = wall_keep(row, rows - 1, parts_y)
    pressure = real_inverse([in_ref[k, :rows, :] for k in range(planes)])
    rim = real_inverse([in_ref[k, rows:, :] for k in range(planes)])
    for z in range(planes):
        here = pl.ds(z, rows, stride=planes)
        p = pressure[z]
        upper = jnp.where(row == rows - 1, rim[z][:1, :], pltpu.roll(p, rows - 1, 0))
        right = jnp.where(lane == cells - 1, row_to_column(rim[z][1:2, :], row, lane), pltpu.roll(p, cells - 1, 1))
        pressure_ref[here, :] = p
        stream_out[here, :] = stream_ref[here, :] - grid_ratio * (right - p)
        normal_out[here, :] = (normal_ref[here, :] - (upper - p)) * keep
        span_out[here, :] = span_ref[here, :] - grid_ratio * (pressure[(z + 1) % planes] - p)


def shape_of(*dims):
    return jax.ShapeDtypeStruct(dims, jnp.float32)


def per_device(stream_vel, normal_vel, span_vel):
    rows, planes, cells = stream_vel.shape
    parts_x, parts_y = lax.axis_size("gx"), lax.axis_size("gy")
    blocks, half = parts_x, parts_x // 2
    if planes != parts_x or rows != half:
        raise ValueError("unsupported sizes")
    turns, inner, outer, decay = tables(planes, cells, blocks, cells * parts_x)
    flat = [a.reshape(rows * planes, cells) for a in (stream_vel, normal_vel, span_vel)]
    scratch = [pltpu.VMEM((2, (rows + 1) * half, cells), jnp.float32), pltpu.VMEM((2 * rows, 2 * cells), jnp.float32)]

    sent = pl.pallas_call(
        functools.partial(source_kernel, planes, parts_y), out_shape=shape_of(planes, 2 * rows, cells), name="source"
    )(*flat)
    taken = lax.all_to_all(sent, "gx", 0, 0)
    sent, modes = pl.pallas_call(
        functools.partial(modes_kernel, rows, parts_y),
        out_shape=(shape_of(parts_y, half, 2 * cells), shape_of(2, (rows + 1) * half, cells)),
        scratch_shapes=scratch,
        name="modes",
    )(taken, turns, inner, outer, decay)
    taken = lax.all_to_all(sent, "gy", 0, 0)
    sent = pl.pallas_call(
        functools.partial(solve_kernel, rows, parts_y),
        out_shape=shape_of(blocks, 2 * rows, cells),
        scratch_shapes=scratch,
        name="solve",
    )(taken, modes, turns, inner, outer, decay)
    taken = lax.all_to_all(sent, "gx", 0, 0)
    outs = pl.pallas_call(
        functools.partial(correct_kernel, parts_y), out_shape=(shape_of(rows * planes, cells),) * 4, name="correct"
    )(taken, *flat)
    return tuple(a.reshape(rows, planes, cells) for a in outs)


def solution(mesh):
    spec = P("gy", None, "gx")
    return jax.shard_map(
        per_device, mesh=mesh, in_specs=(spec,) * 3, out_specs=(spec,) * 4, check_vma=False
    )
```

```python
import functools
import math

import jax
import jax.numpy as jnp
import numpy as np
from jax import lax
from jax.experimental import pallas as pl
from jax.experimental.pallas import tpu as pltpu
from jax.sharding import PartitionSpec as P

shift_term = 1.0 / 1024.0
grid_ratio = 1.0 / 128.0
highest = lax.Precision.HIGHEST


def weighted(terms):
    total = None
    for factor, value in terms:
        if abs(factor) < 1e-12:
            continue
        term = value * factor
        total = term if total is None else total + term
    return total


def angle_tables(count):
    half = count // 2
    cosine = [[math.cos(2 * math.pi * (k * i % count) / count) for i in range(count)] for k in range(half + 1)]
    sine = [[math.sin(2 * math.pi * (k * i % count) / count) for i in range(count)] for k in range(half + 1)]
    return cosine, sine


def real_forward(values):
    count = len(values)
    half = count // 2
    cosine, sine = angle_tables(count)
    even = [values[0]] + [values[i] + values[count - i] for i in range(1, half)] + [values[half]]
    odd = [None] + [values[i] - values[count - i] for i in range(1, half)]
    edge, inner = 1 / math.sqrt(count), math.sqrt(2 / count)
    first = weighted([(edge, value) for value in even])
    middle = weighted([(edge * (-1) ** i, value) for i, value in enumerate(even)])
    cosines = [weighted([(inner * cosine[k][i], even[i]) for i in range(half + 1)]) for k in range(1, half)]
    sines = [weighted([(-inner * sine[k][i], odd[i]) for i in range(1, half)]) for k in range(1, half)]
    return [first, middle, *cosines, *sines]


def real_inverse(planes):
    count = len(planes)
    half = count // 2
    cosine, sine = angle_tables(count)
    edge, inner = 1 / math.sqrt(count), math.sqrt(2 / count)
    values = [None] * count
    for i in range(half + 1):
        even = weighted(
            [(edge, planes[0]), (edge * (-1) ** i, planes[1])]
            + [(inner * cosine[k][i], planes[k + 1]) for k in range(1, half)]
        )
        if i in (0, half):
            values[i] = even
            continue
        odd = weighted([(-inner * sine[k][i], planes[half + k]) for k in range(1, half)])
        values[i] = even + odd
        values[count - i] = even - odd
    return values


def plane_modes(count):
    half = count // 2
    return np.array([0, half, *range(1, half), *range(1, half)])


def tables(planes, lanes, blocks, length_x):
    half = blocks // 2
    t = np.arange(lanes)
    phases = np.arange(half)
    turn = 2 * np.pi * phases[:, None] * t[None, :] / length_x
    turns = np.concatenate([np.cos(turn), np.sin(turn)])
    product = 2 * np.pi * (t[:, None] * t[None, :] % lanes) / lanes
    scale = 1 / math.sqrt(lanes)
    c, s = np.cos(product) * scale, np.sin(product) * scale
    inner = np.block([[c, -s], [s, c]])
    root = math.sqrt(2.0)
    n = lanes // 2
    first = np.concatenate([c[:, :1], root * c[:, 1:n], c[:, n : n + 1], -root * s[:, 1:n]], axis=1)
    shifted = np.pi * (t[:, None] * (2 * np.arange(n)[None, :] + 1) % (2 * lanes)) / lanes
    middle = root * scale * np.concatenate([np.cos(shifted), -np.sin(shifted)], axis=1)
    zero = np.zeros((lanes, lanes))
    outer = np.block([[first, zero], [zero, middle]])
    mode_x = np.zeros((half, 2 * lanes))
    mode_x[1:] = phases[1:, None] + blocks * np.concatenate([t, t])[None, :]
    mode_x[0, : n + 1] = blocks * np.arange(n + 1)
    mode_x[0, n + 1 : lanes] = blocks * np.arange(1, n)
    mode_x[0, lanes:] = half + blocks * np.concatenate([np.arange(n), np.arange(n)])
    wave_x = (2 * np.sin(np.pi * mode_x / length_x)) ** 2
    wave_z = (2 * np.sin(np.pi * plane_modes(planes) / planes)) ** 2
    eigen_sum = grid_ratio * grid_ratio * (wave_z[:, None, None] + wave_x[None]) + shift_term
    decay = 2 * np.arcsinh(np.sqrt(eigen_sum) / 2)
    decay = decay.reshape(planes * half, 2 * lanes)
    turns = np.concatenate([turns[:half], turns[half:]], axis=1)
    return jnp.asarray(np.concatenate([inner, outer]), jnp.float32), jnp.asarray(np.concatenate([decay, turns]), jnp.float32)


class Tables:
    def __init__(self, matrix_ref, ref, lanes, half):
        self.matrix_ref, self.ref, self.lanes, self.half = matrix_ref, ref, lanes, half

    def inner(self):
        return self.matrix_ref[: 2 * self.lanes, :]

    def outer(self):
        return self.matrix_ref[2 * self.lanes :, :]

    def decay(self):
        return self.ref[: self.half, :]

    def turn(self, a):
        line = self.half + a
        return self.ref[line : line + 1, : self.lanes], self.ref[line : line + 1, self.lanes :]


def places(shape):
    return lax.broadcasted_iota(jnp.int32, shape, 0), lax.broadcasted_iota(jnp.int32, shape, 1)


def column_to_row(column, row, lane):
    return jnp.sum(jnp.where(row == lane, column, 0.0), axis=0, keepdims=True)


def row_to_column(line, row, lane):
    return jnp.sum(jnp.where(row == lane, line, 0.0), axis=1, keepdims=True)


def wall_keep(row, last_row, parts_y):
    is_wall = jnp.logical_and(row == last_row, lax.axis_index("gy") == parts_y - 1)
    return jnp.where(is_wall, 0.0, 1.0)


def source_kernel(
    planes, parts_y, stream_hbm, normal_hbm, span_hbm, table_hbm, out_ref, local_ref, stream_ref, normal_ref, span_ref, done
):
    half = local_ref.shape[0] // 2
    decay_rows = pl.ds(pl.multiple_of(lax.axis_index("gx") * half, half), half)
    turn_rows = pl.ds(table_hbm.shape[0] - half, half)
    copies = [
        pltpu.make_async_copy(stream_hbm, stream_ref, done.at[0]),
        pltpu.make_async_copy(normal_hbm, normal_ref, done.at[1]),
        pltpu.make_async_copy(span_hbm, span_ref, done.at[2]),
        pltpu.make_async_copy(table_hbm.at[decay_rows, :], local_ref.at[:half, :], done.at[3]),
        pltpu.make_async_copy(table_hbm.at[turn_rows, :], local_ref.at[half:, :], done.at[4]),
    ]
    for copy in copies:
        copy.start()
    for copy in copies[:3]:
        copy.wait()
    cells = stream_ref.shape[1]
    rows = stream_ref.shape[0] // planes
    row, lane = places((rows, cells))
    keep = wall_keep(row, rows - 1, parts_y)

    def plane(ref, z):
        return ref[pl.ds(z, rows, stride=planes), :]

    main, rim = [], []
    span_before = plane(span_ref, planes - 1)
    for z in range(planes):
        stream, normal, span = plane(stream_ref, z), plane(normal_ref, z) * keep, plane(span_ref, z)
        stream_left = jnp.where(lane == 0, 0.0, pltpu.roll(stream, 1, 1))
        normal_turned = pltpu.roll(normal, 1, 0)
        normal_below = jnp.where(row == 0, 0.0, normal_turned)
        main.append(
            grid_ratio * (stream - stream_left) + (normal - normal_below) + grid_ratio * (span - span_before)
        )
        ends = column_to_row(stream[:, cells - 1 :], row, lane)
        rim.append(jnp.where(row == 0, -normal_turned, jnp.where(row == 1, -grid_ratio * ends, 0.0)))
        span_before = span
    main, rim = real_forward(main), real_forward(rim)
    for k in range(planes):
        out_ref[k, :rows, :] = main[k]
        out_ref[k, rows:, :] = rim[k]
    for copy in copies[3:]:
        copy.wait()


class Line:
    def __init__(self, decay, rows, parts_y):
        base = (lax.axis_index("gy") * rows).astype(jnp.float32)
        total = rows * parts_y
        self.step = jnp.exp(-decay)
        square, grown = self.step * self.step, jnp.exp(2.0 * decay)
        low = jnp.exp(-decay * (2.0 * base + 1.0))
        high = jnp.exp(-decay * (2.0 * (total - base) - 1.0))
        self.low, self.high = [], []
        for _ in range(rows + 1):
            self.low.append(1.0 + low)
            self.high.append(1.0 + high)
            low, high = low * square, high * grown
        self.decay, self.total = decay, total

    def gain(self):
        return -1.0 / ((jnp.exp(self.decay) - self.step) * (1.0 - jnp.exp(self.decay * (-2.0 * self.total))))


def modes_kernel(rows, parts_y, in_ref, matrix_ref, table_ref, send_ref, modes_ref, left, edge):
    blocks, _, lanes = in_ref.shape
    half = blocks // 2
    table = Tables(matrix_ref, table_ref, lanes, half)
    row, lane = places((rows, lanes))
    main = [in_ref[d, :rows, :] for d in range(blocks)]
    rim = [in_ref[d, rows:, :] for d in range(blocks)]
    for d in range(blocks):
        ends = row_to_column(rim[d - 1][1:2, :], row, lane)
        main[d] = main[d] + jnp.where(lane == 0, ends, 0.0)
    main = real_forward(main)
    rim = real_forward([piece[:1, :] for piece in rim])
    edge[...] = jnp.zeros_like(edge)
    for h in range(2):
        edge[:rows, h * lanes : (h + 1) * lanes] = main[h]
        edge[rows : rows + 1, h * lanes : (h + 1) * lanes] = rim[h]
        left[h, pl.ds(0, rows, stride=half), :] = main[h]
        left[h, rows * half : rows * half + 1, :] = rim[h]
    for a in range(1, half):
        c, s = table.turn(a)
        for first, count, (re, im) in (
            (a, rows, (main[a + 1], main[half + a])),
            (rows * half + a, 1, (rim[a + 1], rim[half + a])),
        ):
            left[0, pl.ds(first, count, stride=half), :] = re * c + im * s
            left[1, pl.ds(first, count, stride=half), :] = im * c - re * s
    inner = jnp.dot(
        jnp.concatenate([left[0], left[1]], axis=1), table.inner(), precision=highest, preferred_element_type=jnp.float32
    )
    outer = jnp.dot(edge[...], table.outer(), precision=highest, preferred_element_type=jnp.float32)
    for h in range(2):
        part = slice(h * lanes, (h + 1) * lanes)
        modes_ref[h, :, :] = inner[:, part]
        modes_ref[h, pl.ds(0, rows, stride=half), :] = outer[:rows, part]
        modes_ref[h, rows * half : rows * half + 1, :] = outer[rows : rows + 1, part]
    spectrum = row_list(modes_ref, rows, half)
    line = Line(table.decay(), rows, parts_y)
    below = line.low[0] * spectrum[0]
    above = line.high[rows] * spectrum[rows]
    for i in range(1, rows + 1):
        below = line.low[i] * spectrum[i] + line.step * below
        above = line.high[rows - i] * spectrum[rows - i] + line.step * above
    mine = lax.axis_index("gy")
    for other in range(parts_y):
        send_ref[other, :, :] = jnp.where(mine < other, below, above)


def row_list(modes_ref, rows, half):
    return [
        jnp.concatenate([modes_ref[h, i * half : (i + 1) * half, :] for h in range(2)], axis=1)
        for i in range(rows + 1)
    ]


def entering(pieces_ref, mine, step, group):
    count = pieces_ref.shape[0]
    zero = jnp.zeros_like(step)
    below = above = zero
    for first in range(0, count, group):
        part = zero
        kept = jnp.ones_like(step)
        for i in range(first, min(first + group, count)):
            part = jnp.where(i < mine, pieces_ref[i] + step * part, part)
            kept = jnp.where(i < mine, step * kept, kept)
        below = part + kept * below
        part = zero
        kept = jnp.ones_like(step)
        for i in range(first, min(first + group, count)):
            j = count - 1 - i
            part = jnp.where(j > mine, pieces_ref[j] + step * part, part)
            kept = jnp.where(j > mine, step * kept, kept)
        above = part + kept * above
    return below, above


def solve_kernel(rows, parts_y, in_ref, modes_ref, matrix_ref, table_ref, out_ref, left, edge):
    blocks, _, lanes = out_ref.shape
    half = blocks // 2
    table = Tables(matrix_ref, table_ref, lanes, half)
    row, lane = places((rows, lanes))
    decay = table.decay()
    below, above = entering(in_ref, lax.axis_index("gy"), jnp.exp(-rows * decay), 8)
    line = Line(decay, rows, parts_y)
    spectrum = row_list(modes_ref, rows, half)
    gain = line.gain()
    from_below = [line.low[0] * spectrum[0] + below]
    for i in range(1, rows + 1):
        from_below.append(line.low[i] * spectrum[i] + line.step * from_below[-1])
    from_above = above
    edge[...] = jnp.zeros_like(edge)
    for i in reversed(range(rows + 1)):
        solved = gain * (line.high[i] * from_below[i] + line.low[i] * from_above)
        edge[i : i + 1, :] = solved[:1, :]
        for h in range(2):
            left[h, i * half : (i + 1) * half, :] = solved[:, h * lanes : (h + 1) * lanes]
        from_above = line.step * (from_above + line.high[i] * spectrum[i])
    back = (((1,), (1,)), ((), ()))
    inner = lax.dot_general(
        jnp.concatenate([left[0], left[1]], axis=1),
        table.inner(),
        back,
        precision=highest,
        preferred_element_type=jnp.float32,
    )
    outer = lax.dot_general(
        edge[...], table.outer(), back, precision=highest, preferred_element_type=jnp.float32
    )
    for h in range(2):
        left[h, :, :] = inner[:, h * lanes : (h + 1) * lanes]
    main = [outer[:rows, :lanes], outer[:rows, lanes:]] + [None] * (blocks - 2)
    rim = [outer[rows : rows + 1, :lanes], outer[rows : rows + 1, lanes:]] + [None] * (blocks - 2)
    for a in range(1, half):
        c, s = table.turn(a)
        for planes, first, count in ((main, a, rows), (rim, rows * half + a, 1)):
            re = left[0, pl.ds(first, count, stride=half), :]
            im = left[1, pl.ds(first, count, stride=half), :]
            planes[a + 1] = re * c - im * s
            planes[half + a] = im * c + re * s
    main, rim = real_inverse(main), real_inverse(rim)
    for d in range(blocks):
        out_ref[d, :rows, :] = main[d]
        ends = column_to_row(main[(d + 1) % blocks][:, :1], row, lane)
        out_ref[d, rows:, :] = jnp.where(row == 0, rim[d], jnp.where(row == 1, ends, 0.0))


def correct_kernel(
    parts_y, in_ref, stream_ref, normal_ref, span_ref, pressure_ref, stream_out, normal_out, span_out
):
    planes, _, cells = in_ref.shape
    rows = stream_ref.shape[0] // planes
    row, lane = places((rows, cells))
    keep = wall_keep(row, rows - 1, parts_y)
    pressure = real_inverse([in_ref[k, :rows, :] for k in range(planes)])
    rim = real_inverse([in_ref[k, rows:, :] for k in range(planes)])
    for z in range(planes):
        here = pl.ds(z, rows, stride=planes)
        p = pressure[z]
        upper = jnp.where(row == rows - 1, rim[z][:1, :], pltpu.roll(p, rows - 1, 0))
        right = jnp.where(lane == cells - 1, row_to_column(rim[z][1:2, :], row, lane), pltpu.roll(p, cells - 1, 1))
        pressure_ref[here, :] = p
        stream_out[here, :] = stream_ref[here, :] - grid_ratio * (right - p)
        normal_out[here, :] = (normal_ref[here, :] - (upper - p)) * keep
        span_out[here, :] = span_ref[here, :] - grid_ratio * (pressure[(z + 1) % planes] - p)


def shape_of(*dims):
    return jax.ShapeDtypeStruct(dims, jnp.float32)


def per_device(stream_vel, normal_vel, span_vel):
    rows, planes, cells = stream_vel.shape
    parts_x, parts_y = lax.axis_size("gx"), lax.axis_size("gy")
    blocks, half = parts_x, parts_x // 2
    if planes != parts_x or rows != half:
        raise ValueError("unsupported sizes")
    matrices, table = tables(planes, cells, blocks, cells * parts_x)
    flat = [a.reshape(rows * planes, cells) for a in (stream_vel, normal_vel, span_vel)]
    room = pltpu.CompilerParams(vmem_limit_bytes=8 << 20)
    scratch = [pltpu.VMEM((2, (rows + 1) * half, cells), jnp.float32), pltpu.VMEM((2 * rows, 2 * cells), jnp.float32)]

    sent, local = pl.pallas_call(
        functools.partial(source_kernel, planes, parts_y),
        out_shape=(shape_of(planes, 2 * rows, cells), shape_of(2 * half, 2 * cells)),
        in_specs=[pl.BlockSpec(memory_space=pltpu.HBM)] * 4,
        scratch_shapes=[pltpu.VMEM((rows * planes, cells), jnp.float32)] * 3 + [pltpu.SemaphoreType.DMA((5,))],
        compiler_params=room,
        name="source",
    )(*(pltpu.with_memory_space_constraint(a, pltpu.HBM) for a in (*flat, table)))
    taken = lax.all_to_all(sent, "gx", 0, 0)
    sent, modes = pl.pallas_call(
        functools.partial(modes_kernel, rows, parts_y),
        out_shape=(shape_of(parts_y, half, 2 * cells), shape_of(2, (rows + 1) * half, cells)),
        scratch_shapes=scratch,
        compiler_params=room,
        name="modes",
    )(taken, matrices, local)
    taken = lax.all_to_all(sent, "gy", 0, 0)
    sent = pl.pallas_call(
        functools.partial(solve_kernel, rows, parts_y),
        out_shape=shape_of(blocks, 2 * rows, cells),
        scratch_shapes=scratch,
        compiler_params=room,
        name="solve",
    )(taken, modes, matrices, local)
    taken = lax.all_to_all(sent, "gx", 0, 0)
    outs = pl.pallas_call(
        functools.partial(correct_kernel, parts_y),
        out_shape=(shape_of(rows * planes, cells),) * 4,
        compiler_params=room,
        name="correct",
    )(taken, *flat)
    return tuple(a.reshape(rows, planes, cells) for a in outs)


def solution(mesh):
    spec = P("gy", None, "gx")
    return jax.shard_map(
        per_device, mesh=mesh, in_specs=(spec,) * 3, out_specs=(spec,) * 4, check_vma=False
    )
```

```python
import functools
import math

import jax
import jax.numpy as jnp
import numpy as np
from jax import lax
from jax.experimental import pallas as pl
from jax.experimental.pallas import tpu as pltpu
from jax.sharding import PartitionSpec as P

shift_term = 1.0 / 1024.0
grid_ratio = 1.0 / 128.0
highest = lax.Precision.HIGHEST


def weighted(terms):
    total = None
    for factor, value in terms:
        if abs(factor) < 1e-12:
            continue
        term = value * factor
        total = term if total is None else total + term
    return total


def angle_tables(count):
    half = count // 2
    cosine = [[math.cos(2 * math.pi * (k * i % count) / count) for i in range(count)] for k in range(half + 1)]
    sine = [[math.sin(2 * math.pi * (k * i % count) / count) for i in range(count)] for k in range(half + 1)]
    return cosine, sine


def real_forward(values):
    count = len(values)
    half = count // 2
    cosine, sine = angle_tables(count)
    even = [values[0]] + [values[i] + values[count - i] for i in range(1, half)] + [values[half]]
    odd = [None] + [values[i] - values[count - i] for i in range(1, half)]
    edge, inner = 1 / math.sqrt(count), math.sqrt(2 / count)
    first = weighted([(edge, value) for value in even])
    middle = weighted([(edge * (-1) ** i, value) for i, value in enumerate(even)])
    cosines = [weighted([(inner * cosine[k][i], even[i]) for i in range(half + 1)]) for k in range(1, half)]
    sines = [weighted([(-inner * sine[k][i], odd[i]) for i in range(1, half)]) for k in range(1, half)]
    return [first, middle, *cosines, *sines]


def real_inverse(planes):
    count = len(planes)
    half = count // 2
    cosine, sine = angle_tables(count)
    edge, inner = 1 / math.sqrt(count), math.sqrt(2 / count)
    values = [None] * count
    for i in range(half + 1):
        even = weighted(
            [(edge, planes[0]), (edge * (-1) ** i, planes[1])]
            + [(inner * cosine[k][i], planes[k + 1]) for k in range(1, half)]
        )
        if i in (0, half):
            values[i] = even
            continue
        odd = weighted([(-inner * sine[k][i], planes[half + k]) for k in range(1, half)])
        values[i] = even + odd
        values[count - i] = even - odd
    return values


def plane_modes(count):
    half = count // 2
    return np.array([0, half, *range(1, half), *range(1, half)])


def tables(planes, lanes, blocks, length_x):
    half = blocks // 2
    t = np.arange(lanes)
    phases = np.arange(half)
    turn = 2 * np.pi * phases[:, None] * t[None, :] / length_x
    turns = np.concatenate([np.cos(turn), np.sin(turn)])
    product = 2 * np.pi * (t[:, None] * t[None, :] % lanes) / lanes
    scale = 1 / math.sqrt(lanes)
    c, s = np.cos(product) * scale, np.sin(product) * scale
    inner = np.block([[c, -s], [s, c]])
    root = math.sqrt(2.0)
    n = lanes // 2
    first = np.concatenate([c[:, :1], root * c[:, 1:n], c[:, n : n + 1], -root * s[:, 1:n]], axis=1)
    shifted = np.pi * (t[:, None] * (2 * np.arange(n)[None, :] + 1) % (2 * lanes)) / lanes
    middle = root * scale * np.concatenate([np.cos(shifted), -np.sin(shifted)], axis=1)
    zero = np.zeros((lanes, lanes))
    outer = np.block([[first, zero], [zero, middle]])
    mode_x = np.zeros((half, 2 * lanes))
    mode_x[1:] = phases[1:, None] + blocks * np.concatenate([t, t])[None, :]
    mode_x[0, : n + 1] = blocks * np.arange(n + 1)
    mode_x[0, n + 1 : lanes] = blocks * np.arange(1, n)
    mode_x[0, lanes:] = half + blocks * np.concatenate([np.arange(n), np.arange(n)])
    wave_x = (2 * np.sin(np.pi * mode_x / length_x)) ** 2
    wave_z = (2 * np.sin(np.pi * plane_modes(planes) / planes)) ** 2
    eigen_sum = grid_ratio * grid_ratio * (wave_z[:, None, None] + wave_x[None]) + shift_term
    decay = 2 * np.arcsinh(np.sqrt(eigen_sum) / 2)
    decay = decay.reshape(planes * half, 2 * lanes)
    turns = np.concatenate([turns[:half], turns[half:]], axis=1)
    return jnp.asarray(np.concatenate([inner, outer]), jnp.float32), jnp.asarray(np.concatenate([decay, turns]), jnp.float32)


class Tables:
    def __init__(self, matrix_ref, ref, lanes, half):
        self.matrix_ref, self.ref, self.lanes, self.half = matrix_ref, ref, lanes, half

    def inner(self):
        return self.matrix_ref[: 2 * self.lanes, :]

    def outer(self):
        return self.matrix_ref[2 * self.lanes :, :]

    def decay(self):
        return self.ref[: self.half, :]

    def turn(self, a):
        line = self.half + a
        return self.ref[line : line + 1, : self.lanes], self.ref[line : line + 1, self.lanes :]


def places(shape):
    return lax.broadcasted_iota(jnp.int32, shape, 0), lax.broadcasted_iota(jnp.int32, shape, 1)


def column_to_row(column, row, lane):
    return jnp.sum(jnp.where(row == lane, column, 0.0), axis=0, keepdims=True)


def row_to_column(line, row, lane):
    return jnp.sum(jnp.where(row == lane, line, 0.0), axis=1, keepdims=True)


def wall_keep(row, last_row, parts_y):
    is_wall = jnp.logical_and(row == last_row, lax.axis_index("gy") == parts_y - 1)
    return jnp.where(is_wall, 0.0, 1.0)


def source_kernel(
    planes, parts_y, stream_hbm, normal_hbm, span_hbm, table_hbm, out_ref, local_ref, stream_ref, normal_ref, span_ref, done
):
    half = local_ref.shape[0] // 2
    decay_rows = pl.ds(pl.multiple_of(lax.axis_index("gx") * half, half), half)
    turn_rows = pl.ds(table_hbm.shape[0] - half, half)
    copies = [
        pltpu.make_async_copy(stream_hbm, stream_ref, done.at[0]),
        pltpu.make_async_copy(normal_hbm, normal_ref, done.at[1]),
        pltpu.make_async_copy(span_hbm, span_ref, done.at[2]),
        pltpu.make_async_copy(table_hbm.at[decay_rows, :], local_ref.at[:half, :], done.at[3]),
        pltpu.make_async_copy(table_hbm.at[turn_rows, :], local_ref.at[half:, :], done.at[4]),
    ]
    for copy in copies:
        copy.start()
    for copy in copies[:3]:
        copy.wait()
    cells = stream_ref.shape[1]
    rows = stream_ref.shape[0] // planes
    row, lane = places((rows, cells))
    keep = wall_keep(row, rows - 1, parts_y)

    def plane(ref, z):
        return ref[pl.ds(z, rows, stride=planes), :]

    main, rim = [], []
    span_before = plane(span_ref, planes - 1)
    for z in range(planes):
        stream, normal, span = plane(stream_ref, z), plane(normal_ref, z) * keep, plane(span_ref, z)
        stream_left = jnp.where(lane == 0, 0.0, pltpu.roll(stream, 1, 1))
        normal_turned = pltpu.roll(normal, 1, 0)
        normal_below = jnp.where(row == 0, 0.0, normal_turned)
        main.append(
            grid_ratio * (stream - stream_left) + (normal - normal_below) + grid_ratio * (span - span_before)
        )
        ends = column_to_row(stream[:, cells - 1 :], row, lane)
        rim.append(jnp.where(row == 0, -normal_turned, jnp.where(row == 1, -grid_ratio * ends, 0.0)))
        span_before = span
    main, rim = real_forward(main), real_forward(rim)
    for k in range(planes):
        out_ref[k, :rows, :] = main[k]
        out_ref[k, rows:, :] = rim[k]
    for copy in copies[3:]:
        copy.wait()


class Line:
    def __init__(self, decay, rows, parts_y):
        base = (lax.axis_index("gy") * rows).astype(jnp.float32)
        total = rows * parts_y
        self.step = jnp.exp(-decay)
        square, grown = self.step * self.step, jnp.exp(2.0 * decay)
        low = jnp.exp(-decay * (2.0 * base + 1.0))
        high = jnp.exp(-decay * (2.0 * (total - base) - 1.0))
        self.low, self.high = [], []
        for _ in range(rows + 1):
            self.low.append(1.0 + low)
            self.high.append(1.0 + high)
            low, high = low * square, high * grown
        self.decay, self.total = decay, total

    def gain(self):
        return -1.0 / ((jnp.exp(self.decay) - self.step) * (1.0 - jnp.exp(self.decay * (-2.0 * self.total))))


def modes_kernel(rows, parts_y, in_ref, matrix_ref, table_ref, send_ref, modes_ref, left, edge):
    blocks, _, lanes = in_ref.shape
    half = blocks // 2
    table = Tables(matrix_ref, table_ref, lanes, half)
    row, lane = places((rows, lanes))
    main = [in_ref[d, :rows, :] for d in range(blocks)]
    rim = [in_ref[d, rows:, :] for d in range(blocks)]
    for d in range(blocks):
        ends = row_to_column(rim[d - 1][1:2, :], row, lane)
        main[d] = main[d] + jnp.where(lane == 0, ends, 0.0)
    main = real_forward(main)
    rim = real_forward([piece[:1, :] for piece in rim])
    edge[...] = jnp.zeros_like(edge)
    for h in range(2):
        edge[:rows, h * lanes : (h + 1) * lanes] = main[h]
        edge[rows : rows + 1, h * lanes : (h + 1) * lanes] = rim[h]
        left[h, pl.ds(0, rows, stride=half), :] = main[h]
        left[h, rows * half : rows * half + 1, :] = rim[h]
    for a in range(1, half):
        c, s = table.turn(a)
        for first, count, (re, im) in (
            (a, rows, (main[a + 1], main[half + a])),
            (rows * half + a, 1, (rim[a + 1], rim[half + a])),
        ):
            left[0, pl.ds(first, count, stride=half), :] = re * c + im * s
            left[1, pl.ds(first, count, stride=half), :] = im * c - re * s
    inner = jnp.dot(
        jnp.concatenate([left[0], left[1]], axis=1), table.inner(), precision=highest, preferred_element_type=jnp.float32
    )
    outer = jnp.dot(edge[...], table.outer(), precision=highest, preferred_element_type=jnp.float32)
    for h in range(2):
        part = slice(h * lanes, (h + 1) * lanes)
        modes_ref[h, :, :] = inner[:, part]
        modes_ref[h, pl.ds(0, rows, stride=half), :] = outer[:rows, part]
        modes_ref[h, rows * half : rows * half + 1, :] = outer[rows : rows + 1, part]
    spectrum = row_list(modes_ref, rows, half)
    line = Line(table.decay(), rows, parts_y)
    below = line.low[0] * spectrum[0]
    above = line.high[rows] * spectrum[rows]
    for i in range(1, rows + 1):
        below = line.low[i] * spectrum[i] + line.step * below
        above = line.high[rows - i] * spectrum[rows - i] + line.step * above
    for other in range(send_ref.shape[0]):
        send_ref[other, :half, :] = below
        send_ref[other, half:, :] = above


def row_list(modes_ref, rows, half):
    return [
        jnp.concatenate([modes_ref[h, i * half : (i + 1) * half, :] for h in range(2)], axis=1)
        for i in range(rows + 1)
    ]


def near_kernel(rows, near, in_ref, table_ref, mine_ref, send_ref):
    half = in_ref.shape[1] // 2
    step = jnp.exp(-rows * table_ref[:half, :])
    place, group = lax.rem(lax.axis_index("gy"), near), lax.div(lax.axis_index("gy"), near)
    below = above = jnp.zeros_like(step)
    for i in range(near):
        j = near - 1 - i
        mine_ref[:half, :] = jnp.where(place == i, below, mine_ref[:half, :]) if i else below
        mine_ref[half:, :] = jnp.where(place == j, above, mine_ref[half:, :]) if i else above
        below = in_ref[i, :half, :] + step * below
        above = in_ref[j, half:, :] + step * above
    for other in range(send_ref.shape[0]):
        send_ref[other, :, :] = jnp.where(group < other, below, above)


def entering(pieces_ref, mine, step):
    count = pieces_ref.shape[0]
    below = above = jnp.zeros_like(step)
    for i in range(count):
        j = count - 1 - i
        below = jnp.where(i < mine, pieces_ref[i] + step * below, below)
        above = jnp.where(j > mine, pieces_ref[j] + step * above, above)
    return below, above


def solve_kernel(rows, parts_y, near, in_ref, mine_ref, modes_ref, matrix_ref, table_ref, out_ref, left, edge):
    blocks, _, lanes = out_ref.shape
    half = blocks // 2
    table = Tables(matrix_ref, table_ref, lanes, half)
    row, lane = places((rows, lanes))
    decay = table.decay()
    place, group = lax.rem(lax.axis_index("gy"), near), lax.div(lax.axis_index("gy"), near)
    far_below, far_above = entering(in_ref, group, jnp.exp(-(rows * near) * decay))
    ahead = (rows * place).astype(jnp.float32)
    below = mine_ref[:half, :] + jnp.exp(-decay * ahead) * far_below
    above = mine_ref[half:, :] + jnp.exp(-decay * (rows * (near - 1) - ahead)) * far_above
    line = Line(decay, rows, parts_y)
    spectrum = row_list(modes_ref, rows, half)
    gain = line.gain()
    from_below = [line.low[0] * spectrum[0] + below]
    for i in range(1, rows + 1):
        from_below.append(line.low[i] * spectrum[i] + line.step * from_below[-1])
    from_above = above
    edge[...] = jnp.zeros_like(edge)
    for i in reversed(range(rows + 1)):
        solved = gain * (line.high[i] * from_below[i] + line.low[i] * from_above)
        edge[i : i + 1, :] = solved[:1, :]
        for h in range(2):
            left[h, i * half : (i + 1) * half, :] = solved[:, h * lanes : (h + 1) * lanes]
        from_above = line.step * (from_above + line.high[i] * spectrum[i])
    back = (((1,), (1,)), ((), ()))
    inner = lax.dot_general(
        jnp.concatenate([left[0], left[1]], axis=1),
        table.inner(),
        back,
        precision=highest,
        preferred_element_type=jnp.float32,
    )
    outer = lax.dot_general(
        edge[...], table.outer(), back, precision=highest, preferred_element_type=jnp.float32
    )
    for h in range(2):
        left[h, :, :] = inner[:, h * lanes : (h + 1) * lanes]
    main = [outer[:rows, :lanes], outer[:rows, lanes:]] + [None] * (blocks - 2)
    rim = [outer[rows : rows + 1, :lanes], outer[rows : rows + 1, lanes:]] + [None] * (blocks - 2)
    for a in range(1, half):
        c, s = table.turn(a)
        for planes, first, count in ((main, a, rows), (rim, rows * half + a, 1)):
            re = left[0, pl.ds(first, count, stride=half), :]
            im = left[1, pl.ds(first, count, stride=half), :]
            planes[a + 1] = re * c - im * s
            planes[half + a] = im * c + re * s
    main, rim = real_inverse(main), real_inverse(rim)
    for d in range(blocks):
        out_ref[d, :rows, :] = main[d]
        ends = column_to_row(main[(d + 1) % blocks][:, :1], row, lane)
        out_ref[d, rows:, :] = jnp.where(row == 0, rim[d], jnp.where(row == 1, ends, 0.0))


def correct_kernel(
    parts_y, in_ref, stream_ref, normal_ref, span_ref, pressure_ref, stream_out, normal_out, span_out
):
    planes, _, cells = in_ref.shape
    rows = stream_ref.shape[0] // planes
    row, lane = places((rows, cells))
    keep = wall_keep(row, rows - 1, parts_y)
    pressure = real_inverse([in_ref[k, :rows, :] for k in range(planes)])
    rim = real_inverse([in_ref[k, rows:, :] for k in range(planes)])
    for z in range(planes):
        here = pl.ds(z, rows, stride=planes)
        p = pressure[z]
        upper = jnp.where(row == rows - 1, rim[z][:1, :], pltpu.roll(p, rows - 1, 0))
        right = jnp.where(lane == cells - 1, row_to_column(rim[z][1:2, :], row, lane), pltpu.roll(p, cells - 1, 1))
        pressure_ref[here, :] = p
        stream_out[here, :] = stream_ref[here, :] - grid_ratio * (right - p)
        normal_out[here, :] = (normal_ref[here, :] - (upper - p)) * keep
        span_out[here, :] = span_ref[here, :] - grid_ratio * (pressure[(z + 1) % planes] - p)


def shape_of(*dims):
    return jax.ShapeDtypeStruct(dims, jnp.float32)


def per_device(stream_vel, normal_vel, span_vel):
    rows, planes, cells = stream_vel.shape
    parts_x, parts_y = lax.axis_size("gx"), lax.axis_size("gy")
    blocks, half = parts_x, parts_x // 2
    near = 1 << (parts_y.bit_length() // 2)
    far = parts_y // near
    if planes != parts_x or rows != half or near * far != parts_y:
        raise ValueError("unsupported sizes")
    matrices, table = tables(planes, cells, blocks, cells * parts_x)
    near_groups = [[i * near + k for k in range(near)] for i in range(far)]
    far_groups = [[i + k * near for k in range(far)] for i in range(near)]
    flat = [a.reshape(rows * planes, cells) for a in (stream_vel, normal_vel, span_vel)]
    room = pltpu.CompilerParams(vmem_limit_bytes=8 << 20)
    scratch = [pltpu.VMEM((2, (rows + 1) * half, cells), jnp.float32), pltpu.VMEM((2 * rows, 2 * cells), jnp.float32)]

    sent, local = pl.pallas_call(
        functools.partial(source_kernel, planes, parts_y),
        out_shape=(shape_of(planes, 2 * rows, cells), shape_of(2 * half, 2 * cells)),
        in_specs=[pl.BlockSpec(memory_space=pltpu.HBM)] * 4,
        scratch_shapes=[pltpu.VMEM((rows * planes, cells), jnp.float32)] * 3 + [pltpu.SemaphoreType.DMA((5,))],
        compiler_params=room,
        name="source",
    )(*(pltpu.with_memory_space_constraint(a, pltpu.HBM) for a in (*flat, table)))
    taken = lax.all_to_all(sent, "gx", 0, 0)
    sent, modes = pl.pallas_call(
        functools.partial(modes_kernel, rows, parts_y),
        out_shape=(shape_of(near, 2 * half, 2 * cells), shape_of(2, (rows + 1) * half, cells)),
        scratch_shapes=scratch,
        compiler_params=room,
        name="modes",
    )(taken, matrices, local)
    taken = lax.all_to_all(sent, "gy", 0, 0, axis_index_groups=near_groups)
    mine, sent = pl.pallas_call(
        functools.partial(near_kernel, rows, near),
        out_shape=(shape_of(2 * half, 2 * cells), shape_of(far, half, 2 * cells)),
        compiler_params=room,
        name="near",
    )(taken, local)
    taken = lax.all_to_all(sent, "gy", 0, 0, axis_index_groups=far_groups)
    sent = pl.pallas_call(
        functools.partial(solve_kernel, rows, parts_y, near),
        out_shape=shape_of(blocks, 2 * rows, cells),
        scratch_shapes=scratch,
        compiler_params=room,
        name="solve",
    )(taken, mine, modes, matrices, local)
    taken = lax.all_to_all(sent, "gx", 0, 0)
    outs = pl.pallas_call(
        functools.partial(correct_kernel, parts_y),
        out_shape=(shape_of(rows * planes, cells),) * 4,
        compiler_params=room,
        name="correct",
    )(taken, *flat)
    return tuple(a.reshape(rows, planes, cells) for a in outs)


def solution(mesh):
    spec = P("gy", None, "gx")
    return jax.shard_map(
        per_device, mesh=mesh, in_specs=(spec,) * 3, out_specs=(spec,) * 4, check_vma=False
    )
```

```python
import functools
import math

import jax
import jax.numpy as jnp
import numpy as np
from jax import lax
from jax.experimental import pallas as pl
from jax.experimental.pallas import tpu as pltpu
from jax.sharding import PartitionSpec as P

shift_term = 1.0 / 1024.0
grid_ratio = 1.0 / 128.0
highest = lax.Precision.HIGHEST


def weighted(terms):
    total = None
    for factor, value in terms:
        if abs(factor) < 1e-12:
            continue
        term = value * factor
        total = term if total is None else total + term
    return total


def angle_tables(count):
    half = count // 2
    cosine = [[math.cos(2 * math.pi * (k * i % count) / count) for i in range(count)] for k in range(half + 1)]
    sine = [[math.sin(2 * math.pi * (k * i % count) / count) for i in range(count)] for k in range(half + 1)]
    return cosine, sine


def real_forward(values):
    count = len(values)
    half = count // 2
    cosine, sine = angle_tables(count)
    even = [values[0]] + [values[i] + values[count - i] for i in range(1, half)] + [values[half]]
    odd = [None] + [values[i] - values[count - i] for i in range(1, half)]
    edge, inner = 1 / math.sqrt(count), math.sqrt(2 / count)
    first = weighted([(edge, value) for value in even])
    middle = weighted([(edge * (-1) ** i, value) for i, value in enumerate(even)])
    cosines = [weighted([(inner * cosine[k][i], even[i]) for i in range(half + 1)]) for k in range(1, half)]
    sines = [weighted([(-inner * sine[k][i], odd[i]) for i in range(1, half)]) for k in range(1, half)]
    return [first, middle, *cosines, *sines]


def real_inverse(planes):
    count = len(planes)
    half = count // 2
    cosine, sine = angle_tables(count)
    edge, inner = 1 / math.sqrt(count), math.sqrt(2 / count)
    values = [None] * count
    for i in range(half + 1):
        even = weighted(
            [(edge, planes[0]), (edge * (-1) ** i, planes[1])]
            + [(inner * cosine[k][i], planes[k + 1]) for k in range(1, half)]
        )
        if i in (0, half):
            values[i] = even
            continue
        odd = weighted([(-inner * sine[k][i], planes[half + k]) for k in range(1, half)])
        values[i] = even + odd
        values[count - i] = even - odd
    return values


def plane_modes(count):
    half = count // 2
    return np.array([0, half, *range(1, half), *range(1, half)])


def tables(planes, lanes, blocks, length_x):
    half = blocks // 2
    t = np.arange(lanes)
    phases = np.arange(half)
    turn = 2 * np.pi * phases[:, None] * t[None, :] / length_x
    turns = np.concatenate([np.cos(turn), np.sin(turn)])
    product = 2 * np.pi * (t[:, None] * t[None, :] % lanes) / lanes
    scale = 1 / math.sqrt(lanes)
    c, s = np.cos(product) * scale, np.sin(product) * scale
    inner = np.block([[c, -s], [s, c]])
    root = math.sqrt(2.0)
    n = lanes // 2
    first = np.concatenate([c[:, :1], root * c[:, 1:n], c[:, n : n + 1], -root * s[:, 1:n]], axis=1)
    shifted = np.pi * (t[:, None] * (2 * np.arange(n)[None, :] + 1) % (2 * lanes)) / lanes
    middle = root * scale * np.concatenate([np.cos(shifted), -np.sin(shifted)], axis=1)
    zero = np.zeros((lanes, lanes))
    outer = np.block([[first, zero], [zero, middle]])
    mode_x = np.zeros((half, 2 * lanes))
    mode_x[1:] = phases[1:, None] + blocks * np.concatenate([t, t])[None, :]
    mode_x[0, : n + 1] = blocks * np.arange(n + 1)
    mode_x[0, n + 1 : lanes] = blocks * np.arange(1, n)
    mode_x[0, lanes:] = half + blocks * np.concatenate([np.arange(n), np.arange(n)])
    wave_x = (2 * np.sin(np.pi * mode_x / length_x)) ** 2
    wave_z = (2 * np.sin(np.pi * plane_modes(planes) / planes)) ** 2
    eigen_sum = grid_ratio * grid_ratio * (wave_z[:, None, None] + wave_x[None]) + shift_term
    decay = 2 * np.arcsinh(np.sqrt(eigen_sum) / 2)
    decay = decay.reshape(planes * half, 2 * lanes)
    turns = np.concatenate([turns[:half], turns[half:]], axis=1)
    return jnp.asarray(np.concatenate([inner, outer]), jnp.float32), jnp.asarray(np.concatenate([decay, turns]), jnp.float32)


class Tables:
    def __init__(self, matrix_ref, ref, lanes, half):
        self.matrix_ref, self.ref, self.lanes, self.half = matrix_ref, ref, lanes, half

    def inner(self):
        return self.matrix_ref[: 2 * self.lanes, :]

    def outer(self):
        return self.matrix_ref[2 * self.lanes :, :]

    def decay(self):
        return self.ref[: self.half, :]

    def turn(self, a):
        line = self.half + a
        return self.ref[line : line + 1, : self.lanes], self.ref[line : line + 1, self.lanes :]


def places(shape):
    return lax.broadcasted_iota(jnp.int32, shape, 0), lax.broadcasted_iota(jnp.int32, shape, 1)


def column_to_row(column, row, lane):
    return jnp.sum(jnp.where(row == lane, column, 0.0), axis=0, keepdims=True)


def row_to_column(line, row, lane):
    return jnp.sum(jnp.where(row == lane, line, 0.0), axis=1, keepdims=True)


def wall_keep(row, last_row, parts_y):
    is_wall = jnp.logical_and(row == last_row, lax.axis_index("gy") == parts_y - 1)
    return jnp.where(is_wall, 0.0, 1.0)


def source_kernel(
    planes,
    parts_y,
    stream_hbm,
    normal_hbm,
    span_hbm,
    table_hbm,
    matrix_hbm,
    out_ref,
    local_ref,
    matrix_ref,
    stream_ref,
    normal_ref,
    span_ref,
    done,
):
    half = local_ref.shape[0] // 2
    decay_rows = pl.ds(pl.multiple_of(lax.axis_index("gx") * half, half), half)
    turn_rows = pl.ds(table_hbm.shape[0] - half, half)
    copies = [
        pltpu.make_async_copy(stream_hbm, stream_ref, done.at[0]),
        pltpu.make_async_copy(normal_hbm, normal_ref, done.at[1]),
        pltpu.make_async_copy(span_hbm, span_ref, done.at[2]),
        pltpu.make_async_copy(table_hbm.at[decay_rows, :], local_ref.at[:half, :], done.at[3]),
        pltpu.make_async_copy(table_hbm.at[turn_rows, :], local_ref.at[half:, :], done.at[4]),
        pltpu.make_async_copy(matrix_hbm, matrix_ref, done.at[5]),
    ]
    for copy in copies:
        copy.start()
    for copy in copies[:3]:
        copy.wait()
    cells = stream_ref.shape[1]
    rows = stream_ref.shape[0] // planes
    row, lane = places((rows, cells))
    keep = wall_keep(row, rows - 1, parts_y)

    def plane(ref, z):
        return ref[pl.ds(z, rows, stride=planes), :]

    main, rim = [], []
    span_before = plane(span_ref, planes - 1)
    for z in range(planes):
        stream, normal, span = plane(stream_ref, z), plane(normal_ref, z) * keep, plane(span_ref, z)
        stream_left = jnp.where(lane == 0, 0.0, pltpu.roll(stream, 1, 1))
        normal_turned = pltpu.roll(normal, 1, 0)
        normal_below = jnp.where(row == 0, 0.0, normal_turned)
        main.append(
            grid_ratio * (stream - stream_left) + (normal - normal_below) + grid_ratio * (span - span_before)
        )
        ends = column_to_row(stream[:, cells - 1 :], row, lane)
        rim.append(jnp.where(row == 0, -normal_turned, jnp.where(row == 1, -grid_ratio * ends, 0.0)))
        span_before = span
    main, rim = real_forward(main), real_forward(rim)
    for k in range(planes):
        put(out_ref, k, main[k], rim[k])
    for copy in copies[3:]:
        copy.wait()


def put(ref, index, main, rim):
    pairs = ref.shape[1] - 1
    for j in range(pairs):
        ref[index, j] = main[2 * j : 2 * j + 2, :]
    ref[index, pairs] = rim[:2, :]


def take(ref, held):
    count, pairs = ref.shape[0], ref.shape[1] - 1
    for i in range(count):
        for j in range(pairs):
            held[i, 2 * j : 2 * j + 2, :] = ref[i, j]
    return [held[i] for i in range(count)], [ref[i, pairs] for i in range(count)]


class Line:
    def __init__(self, decay, rows, parts_y):
        base = (lax.axis_index("gy") * rows).astype(jnp.float32)
        total = rows * parts_y
        self.step = jnp.exp(-decay)
        square, grown = self.step * self.step, jnp.exp(2.0 * decay)
        low = jnp.exp(-decay * (2.0 * base + 1.0))
        high = jnp.exp(-decay * (2.0 * (total - base) - 1.0))
        self.low, self.high = [], []
        for _ in range(rows + 1):
            self.low.append(1.0 + low)
            self.high.append(1.0 + high)
            low, high = low * square, high * grown
        self.decay, self.total = decay, total

    def gain(self):
        return -1.0 / ((jnp.exp(self.decay) - self.step) * (1.0 - jnp.exp(self.decay * (-2.0 * self.total))))


def modes_kernel(rows, parts_y, in_ref, matrix_ref, table_ref, send_ref, modes_ref, left, edge, held):
    blocks, _, _, lanes = in_ref.shape
    half = blocks // 2
    table = Tables(matrix_ref, table_ref, lanes, half)
    row, lane = places((rows, lanes))
    main, rim = take(in_ref, held)
    for d in range(blocks):
        ends = row_to_column(rim[d - 1][1:2, :], row, lane)
        main[d] = main[d] + jnp.where(lane == 0, ends, 0.0)
    main = real_forward(main)
    rim = real_forward([piece[:1, :] for piece in rim])
    edge[...] = jnp.zeros_like(edge)
    for h in range(2):
        edge[:rows, h * lanes : (h + 1) * lanes] = main[h]
        edge[rows : rows + 1, h * lanes : (h + 1) * lanes] = rim[h]
        left[h, pl.ds(0, rows, stride=half), :] = main[h]
        left[h, rows * half : rows * half + 1, :] = rim[h]
    for a in range(1, half):
        c, s = table.turn(a)
        for first, count, (re, im) in (
            (a, rows, (main[a + 1], main[half + a])),
            (rows * half + a, 1, (rim[a + 1], rim[half + a])),
        ):
            left[0, pl.ds(first, count, stride=half), :] = re * c + im * s
            left[1, pl.ds(first, count, stride=half), :] = im * c - re * s
    inner = jnp.dot(
        jnp.concatenate([left[0], left[1]], axis=1), table.inner(), precision=highest, preferred_element_type=jnp.float32
    )
    outer = jnp.dot(edge[...], table.outer(), precision=highest, preferred_element_type=jnp.float32)
    for h in range(2):
        part = slice(h * lanes, (h + 1) * lanes)
        modes_ref[h, :, :] = inner[:, part]
        modes_ref[h, pl.ds(0, rows, stride=half), :] = outer[:rows, part]
        modes_ref[h, rows * half : rows * half + 1, :] = outer[rows : rows + 1, part]
    spectrum = row_list(modes_ref, rows, half)
    line = Line(table.decay(), rows, parts_y)
    below = line.low[0] * spectrum[0]
    above = line.high[rows] * spectrum[rows]
    for i in range(1, rows + 1):
        below = line.low[i] * spectrum[i] + line.step * below
        above = line.high[rows - i] * spectrum[rows - i] + line.step * above
    for other in range(send_ref.shape[0]):
        send_ref[other, :half, :] = below
        send_ref[other, half:, :] = above


def row_list(modes_ref, rows, half):
    return [
        jnp.concatenate([modes_ref[h, i * half : (i + 1) * half, :] for h in range(2)], axis=1)
        for i in range(rows + 1)
    ]


def near_kernel(rows, near, in_ref, table_ref, mine_ref, send_ref):
    half = in_ref.shape[1] // 2
    step = jnp.exp(-rows * table_ref[:half, :])
    place, group = lax.rem(lax.axis_index("gy"), near), lax.div(lax.axis_index("gy"), near)
    below = above = jnp.zeros_like(step)
    for i in range(near):
        j = near - 1 - i
        mine_ref[:half, :] = jnp.where(place == i, below, mine_ref[:half, :]) if i else below
        mine_ref[half:, :] = jnp.where(place == j, above, mine_ref[half:, :]) if i else above
        below = in_ref[i, :half, :] + step * below
        above = in_ref[j, half:, :] + step * above
    for other in range(send_ref.shape[0]):
        send_ref[other, :, :] = jnp.where(group < other, below, above)


def entering(pieces_ref, mine, step):
    count = pieces_ref.shape[0]
    below = above = jnp.zeros_like(step)
    for i in range(count):
        j = count - 1 - i
        below = jnp.where(i < mine, pieces_ref[i] + step * below, below)
        above = jnp.where(j > mine, pieces_ref[j] + step * above, above)
    return below, above


def solve_kernel(rows, parts_y, near, in_ref, mine_ref, modes_ref, matrix_ref, table_ref, out_ref, left, edge):
    blocks, _, _, lanes = out_ref.shape
    half = blocks // 2
    table = Tables(matrix_ref, table_ref, lanes, half)
    row, lane = places((rows, lanes))
    decay = table.decay()
    place, group = lax.rem(lax.axis_index("gy"), near), lax.div(lax.axis_index("gy"), near)
    far_below, far_above = entering(in_ref, group, jnp.exp(-(rows * near) * decay))
    ahead = (rows * place).astype(jnp.float32)
    below = mine_ref[:half, :] + jnp.exp(-decay * ahead) * far_below
    above = mine_ref[half:, :] + jnp.exp(-decay * (rows * (near - 1) - ahead)) * far_above
    line = Line(decay, rows, parts_y)
    spectrum = row_list(modes_ref, rows, half)
    gain = line.gain()
    from_below = [line.low[0] * spectrum[0] + below]
    for i in range(1, rows + 1):
        from_below.append(line.low[i] * spectrum[i] + line.step * from_below[-1])
    from_above = above
    edge[...] = jnp.zeros_like(edge)
    for i in reversed(range(rows + 1)):
        solved = gain * (line.high[i] * from_below[i] + line.low[i] * from_above)
        edge[i : i + 1, :] = solved[:1, :]
        for h in range(2):
            left[h, i * half : (i + 1) * half, :] = solved[:, h * lanes : (h + 1) * lanes]
        from_above = line.step * (from_above + line.high[i] * spectrum[i])
    back = (((1,), (1,)), ((), ()))
    inner = lax.dot_general(
        jnp.concatenate([left[0], left[1]], axis=1),
        table.inner(),
        back,
        precision=highest,
        preferred_element_type=jnp.float32,
    )
    outer = lax.dot_general(
        edge[...], table.outer(), back, precision=highest, preferred_element_type=jnp.float32
    )
    for h in range(2):
        left[h, :, :] = inner[:, h * lanes : (h + 1) * lanes]
    main = [outer[:rows, :lanes], outer[:rows, lanes:]] + [None] * (blocks - 2)
    rim = [outer[rows : rows + 1, :lanes], outer[rows : rows + 1, lanes:]] + [None] * (blocks - 2)
    for a in range(1, half):
        c, s = table.turn(a)
        for planes, first, count in ((main, a, rows), (rim, rows * half + a, 1)):
            re = left[0, pl.ds(first, count, stride=half), :]
            im = left[1, pl.ds(first, count, stride=half), :]
            planes[a + 1] = re * c - im * s
            planes[half + a] = im * c + re * s
    main, rim = real_inverse(main), real_inverse(rim)
    for d in range(blocks):
        ends = column_to_row(main[(d + 1) % blocks][:, :1], row, lane)
        put(out_ref, d, main[d], jnp.where(row == 0, rim[d], ends))


def correct_kernel(
    parts_y, in_ref, stream_ref, normal_ref, span_ref, pressure_ref, stream_out, normal_out, span_out, held
):
    planes, _, _, cells = in_ref.shape
    rows = stream_ref.shape[0] // planes
    row, lane = places((rows, cells))
    keep = wall_keep(row, rows - 1, parts_y)
    pressure, rim = take(in_ref, held)
    pressure, rim = real_inverse(pressure), real_inverse(rim)
    for z in range(planes):
        here = pl.ds(z, rows, stride=planes)
        p = pressure[z]
        upper = jnp.where(row == rows - 1, rim[z][:1, :], pltpu.roll(p, rows - 1, 0))
        right = jnp.where(lane == cells - 1, row_to_column(rim[z][1:2, :], row, lane), pltpu.roll(p, cells - 1, 1))
        pressure_ref[here, :] = p
        stream_out[here, :] = stream_ref[here, :] - grid_ratio * (right - p)
        normal_out[here, :] = (normal_ref[here, :] - (upper - p)) * keep
        span_out[here, :] = span_ref[here, :] - grid_ratio * (pressure[(z + 1) % planes] - p)


def shape_of(*dims):
    return jax.ShapeDtypeStruct(dims, jnp.float32)


def per_device(stream_vel, normal_vel, span_vel):
    rows, planes, cells = stream_vel.shape
    parts_x, parts_y = lax.axis_size("gx"), lax.axis_size("gy")
    blocks, half = parts_x, parts_x // 2
    near = 1 << (parts_y.bit_length() // 2)
    far = parts_y // near
    if planes != parts_x or rows != half or near * far != parts_y:
        raise ValueError("unsupported sizes")
    matrices, table = tables(planes, cells, blocks, cells * parts_x)
    near_groups = [[i * near + k for k in range(near)] for i in range(far)]
    far_groups = [[i + k * near for k in range(far)] for i in range(near)]
    flat = [a.reshape(rows * planes, cells) for a in (stream_vel, normal_vel, span_vel)]
    message = shape_of(blocks, rows // 2 + 1, 2, cells)
    held = pltpu.VMEM((blocks, rows, cells), jnp.float32)
    room = pltpu.CompilerParams(vmem_limit_bytes=8 << 20)
    scratch = [pltpu.VMEM((2, (rows + 1) * half, cells), jnp.float32), pltpu.VMEM((2 * rows, 2 * cells), jnp.float32)]

    kept = [matrices, *flat]
    sent, local, *kept = pl.pallas_call(
        functools.partial(source_kernel, planes, parts_y),
        out_shape=(message, shape_of(2 * half, 2 * cells), *(shape_of(*a.shape) for a in kept)),
        in_specs=[pl.BlockSpec(memory_space=pltpu.HBM)] * 5,
        scratch_shapes=[pltpu.SemaphoreType.DMA((6,))],
        compiler_params=room,
        name="source",
    )(*(pltpu.with_memory_space_constraint(a, pltpu.HBM) for a in (*flat, table, matrices)))
    matrices, *flat = kept
    taken = lax.all_to_all(sent, "gx", 0, 0)
    sent, modes = pl.pallas_call(
        functools.partial(modes_kernel, rows, parts_y),
        out_shape=(shape_of(near, 2 * half, 2 * cells), shape_of(2, (rows + 1) * half, cells)),
        scratch_shapes=[*scratch, held],
        compiler_params=room,
        name="modes",
    )(taken, matrices, local)
    taken = lax.all_to_all(sent, "gy", 0, 0, axis_index_groups=near_groups)
    mine, sent = pl.pallas_call(
        functools.partial(near_kernel, rows, near),
        out_shape=(shape_of(2 * half, 2 * cells), shape_of(far, half, 2 * cells)),
        compiler_params=room,
        name="near",
    )(taken, local)
    taken = lax.all_to_all(sent, "gy", 0, 0, axis_index_groups=far_groups)
    sent = pl.pallas_call(
        functools.partial(solve_kernel, rows, parts_y, near),
        out_shape=message,
        scratch_shapes=scratch,
        compiler_params=room,
        name="solve",
    )(taken, mine, modes, matrices, local)
    taken = lax.all_to_all(sent, "gx", 0, 0)
    outs = pl.pallas_call(
        functools.partial(correct_kernel, parts_y),
        out_shape=(shape_of(rows * planes, cells),) * 4,
        scratch_shapes=[held],
        compiler_params=room,
        name="correct",
    )(taken, *flat)
    return tuple(a.reshape(rows, planes, cells) for a in outs)


def solution(mesh):
    spec = P("gy", None, "gx")
    return jax.shard_map(
        per_device, mesh=mesh, in_specs=(spec,) * 3, out_specs=(spec,) * 4, check_vma=False
    )
```

```python
import functools
import math

import jax
import jax.numpy as jnp
import ml_dtypes
import numpy as np
from jax import lax
from jax.experimental import pallas as pl
from jax.experimental.pallas import tpu as pltpu
from jax.sharding import PartitionSpec as P

shift_term = 1.0 / 1024.0
grid_ratio = 1.0 / 128.0


def weighted(terms):
    total = None
    for factor, value in terms:
        if abs(factor) < 1e-12:
            continue
        term = value * factor
        total = term if total is None else total + term
    return total


def angle_tables(count):
    half = count // 2
    cosine = [[math.cos(2 * math.pi * (k * i % count) / count) for i in range(count)] for k in range(half + 1)]
    sine = [[math.sin(2 * math.pi * (k * i % count) / count) for i in range(count)] for k in range(half + 1)]
    return cosine, sine


def real_forward(values):
    count = len(values)
    half = count // 2
    cosine, sine = angle_tables(count)
    even = [values[0]] + [values[i] + values[count - i] for i in range(1, half)] + [values[half]]
    odd = [None] + [values[i] - values[count - i] for i in range(1, half)]
    edge, inner = 1 / math.sqrt(count), math.sqrt(2 / count)
    first = weighted([(edge, value) for value in even])
    middle = weighted([(edge * (-1) ** i, value) for i, value in enumerate(even)])
    cosines = [weighted([(inner * cosine[k][i], even[i]) for i in range(half + 1)]) for k in range(1, half)]
    sines = [weighted([(-inner * sine[k][i], odd[i]) for i in range(1, half)]) for k in range(1, half)]
    return [first, middle, *cosines, *sines]


def real_inverse(planes):
    count = len(planes)
    half = count // 2
    cosine, sine = angle_tables(count)
    edge, inner = 1 / math.sqrt(count), math.sqrt(2 / count)
    values = [None] * count
    for i in range(half + 1):
        even = weighted(
            [(edge, planes[0]), (edge * (-1) ** i, planes[1])]
            + [(inner * cosine[k][i], planes[k + 1]) for k in range(1, half)]
        )
        if i in (0, half):
            values[i] = even
            continue
        odd = weighted([(-inner * sine[k][i], planes[half + k]) for k in range(1, half)])
        values[i] = even + odd
        values[count - i] = even - odd
    return values


def plane_modes(count):
    half = count // 2
    return np.array([0, half, *range(1, half), *range(1, half)])


def tables(planes, lanes, blocks, length_x):
    half = blocks // 2
    t = np.arange(lanes)
    phases = np.arange(half)
    turn = 2 * np.pi * phases[:, None] * t[None, :] / length_x
    turns = np.concatenate([np.cos(turn), np.sin(turn)])
    product = 2 * np.pi * (t[:, None] * t[None, :] % lanes) / lanes
    scale = 1 / math.sqrt(lanes)
    c, s = np.cos(product) * scale, np.sin(product) * scale
    inner = np.block([[c, -s], [s, c]])
    root = math.sqrt(2.0)
    n = lanes // 2
    first = np.concatenate([c[:, :1], root * c[:, 1:n], c[:, n : n + 1], -root * s[:, 1:n]], axis=1)
    shifted = np.pi * (t[:, None] * (2 * np.arange(n)[None, :] + 1) % (2 * lanes)) / lanes
    middle = root * scale * np.concatenate([np.cos(shifted), -np.sin(shifted)], axis=1)
    outer = np.concatenate([first, middle], axis=1)
    mode_x = np.zeros((half, 2 * lanes))
    mode_x[1:] = phases[1:, None] + blocks * np.concatenate([t, t])[None, :]
    mode_x[0, : n + 1] = blocks * np.arange(n + 1)
    mode_x[0, n + 1 : lanes] = blocks * np.arange(1, n)
    mode_x[0, lanes:] = half + blocks * np.concatenate([np.arange(n), np.arange(n)])
    wave_x = (2 * np.sin(np.pi * mode_x / length_x)) ** 2
    wave_z = (2 * np.sin(np.pi * plane_modes(planes) / planes)) ** 2
    eigen_sum = grid_ratio * grid_ratio * (wave_z[:, None, None] + wave_x[None]) + shift_term
    decay = 2 * np.arcsinh(np.sqrt(eigen_sum) / 2)
    decay = decay.reshape(planes * half, 2 * lanes)
    turns = np.concatenate([turns[:half], turns[half:]], axis=1)
    matrices = np.concatenate([inner, outer])
    parts = []
    for _ in range(3):
        parts.append(matrices.astype(ml_dtypes.bfloat16))
        matrices = matrices - parts[-1].astype(np.float64)
    return jnp.asarray(np.concatenate(parts)), jnp.asarray(np.concatenate([decay, turns]), jnp.float32)


def split(values, count):
    parts = []
    for _ in range(count):
        parts.append(values.astype(jnp.bfloat16))
        values = values - parts[-1].astype(jnp.float32)
    return parts


def product(values, matrix, transposed=False):
    parts, rows = split(values, len(matrix)), values.shape[0]
    dims = (((1,), (1 if transposed else 0,)), ((), ()))
    terms = []
    for j, piece in enumerate(matrix):
        stacked = parts[: len(parts) - j]
        stacked = jnp.concatenate(stacked) if len(stacked) > 1 else stacked[0]
        terms.append(lax.dot_general(stacked, piece, dims, preferred_element_type=jnp.float32))
    total = None
    for size in reversed(range(len(matrix))):
        for j in range(size + 1):
            i = size - j
            term = terms[j][i * rows : (i + 1) * rows]
            total = term if total is None else total + term
    return total


class Tables:
    def __init__(self, matrix_ref, ref, lanes, half):
        self.matrix_ref, self.ref, self.lanes, self.half = matrix_ref, ref, lanes, half

    def inner(self, parts):
        return [self.matrix_ref[i * 3 * self.lanes : (i * 3 + 2) * self.lanes, :] for i in range(parts)]

    def outer(self, h, parts):
        part = slice(h * self.lanes, (h + 1) * self.lanes)
        return [self.matrix_ref[(i * 3 + 2) * self.lanes : (i * 3 + 3) * self.lanes, part] for i in range(parts)]

    def decay(self):
        return self.ref[: self.half, :]

    def turn(self, a):
        line = self.half + a
        return self.ref[line : line + 1, : self.lanes], self.ref[line : line + 1, self.lanes :]


def places(shape):
    return lax.broadcasted_iota(jnp.int32, shape, 0), lax.broadcasted_iota(jnp.int32, shape, 1)


def column_to_row(column, row, lane):
    return jnp.sum(jnp.where(row == lane, column, 0.0), axis=0, keepdims=True)


def row_to_column(line, row, lane):
    return jnp.sum(jnp.where(row == lane, line, 0.0), axis=1, keepdims=True)


def wall_keep(row, last_row, parts_y):
    is_wall = jnp.logical_and(row == last_row, lax.axis_index("gy") == parts_y - 1)
    return jnp.where(is_wall, 0.0, 1.0)


def source_kernel(
    planes,
    parts_y,
    stream_hbm,
    normal_hbm,
    span_hbm,
    table_hbm,
    matrix_hbm,
    out_ref,
    local_ref,
    matrix_ref,
    stream_ref,
    normal_ref,
    span_ref,
    done,
):
    half = local_ref.shape[0] // 2
    decay_rows = pl.ds(pl.multiple_of(lax.axis_index("gx") * half, half), half)
    turn_rows = pl.ds(table_hbm.shape[0] - half, half)
    copies = [
        pltpu.make_async_copy(stream_hbm, stream_ref, done.at[0]),
        pltpu.make_async_copy(normal_hbm, normal_ref, done.at[1]),
        pltpu.make_async_copy(span_hbm, span_ref, done.at[2]),
        pltpu.make_async_copy(table_hbm.at[decay_rows, :], local_ref.at[:half, :], done.at[3]),
        pltpu.make_async_copy(table_hbm.at[turn_rows, :], local_ref.at[half:, :], done.at[4]),
        pltpu.make_async_copy(matrix_hbm, matrix_ref, done.at[5]),
    ]
    for copy in copies:
        copy.start()
    for copy in copies[:3]:
        copy.wait()
    cells = stream_ref.shape[1]
    rows = stream_ref.shape[0] // planes
    row, lane = places((rows, cells))
    keep = wall_keep(row, rows - 1, parts_y)

    def plane(ref, z):
        return ref[pl.ds(z, rows, stride=planes), :]

    main, rim = [], []
    span_before = plane(span_ref, planes - 1)
    for z in range(planes):
        stream, normal, span = plane(stream_ref, z), plane(normal_ref, z) * keep, plane(span_ref, z)
        stream_left = jnp.where(lane == 0, 0.0, pltpu.roll(stream, 1, 1))
        normal_turned = pltpu.roll(normal, 1, 0)
        normal_below = jnp.where(row == 0, 0.0, normal_turned)
        main.append(
            grid_ratio * (stream - stream_left) + (normal - normal_below) + grid_ratio * (span - span_before)
        )
        ends = column_to_row(stream[:, cells - 1 :], row, lane)
        rim.append(jnp.where(row == 0, -normal_turned, jnp.where(row == 1, -grid_ratio * ends, 0.0)))
        span_before = span
    main, rim = real_forward(main), real_forward(rim)
    for k in range(planes):
        put(out_ref, k, main[k], rim[k])
    for copy in copies[3:]:
        copy.wait()


def put(ref, index, main, rim):
    pairs = ref.shape[1] - 1
    for j in range(pairs):
        ref[index, j] = main[2 * j : 2 * j + 2, :]
    ref[index, pairs] = rim[:2, :]


def take(ref, held):
    count, pairs = ref.shape[0], ref.shape[1] - 1
    for i in range(count):
        for j in range(pairs):
            held[i, 2 * j : 2 * j + 2, :] = ref[i, j]
    return [held[i] for i in range(count)], [ref[i, pairs] for i in range(count)]


class Line:
    def __init__(self, decay, rows, parts_y):
        base = (lax.axis_index("gy") * rows).astype(jnp.float32)
        total = rows * parts_y
        self.step = jnp.exp(-decay)
        square, grown = self.step * self.step, jnp.exp(2.0 * decay)
        low = jnp.exp(-decay * (2.0 * base + 1.0))
        high = jnp.exp(-decay * (2.0 * (total - base) - 1.0))
        self.low, self.high = [], []
        for _ in range(rows + 1):
            self.low.append(1.0 + low)
            self.high.append(1.0 + high)
            low, high = low * square, high * grown
        self.decay, self.total = decay, total

    def gain(self):
        return -1.0 / ((jnp.exp(self.decay) - self.step) * (1.0 - jnp.exp(self.decay * (-2.0 * self.total))))


def modes_kernel(rows, parts_y, in_ref, matrix_ref, table_ref, send_ref, modes_ref, left, edge, held):
    blocks, _, _, lanes = in_ref.shape
    half = blocks // 2
    table = Tables(matrix_ref, table_ref, lanes, half)
    row, lane = places((rows, lanes))
    main, rim = take(in_ref, held)
    for d in range(blocks):
        ends = row_to_column(rim[d - 1][1:2, :], row, lane)
        main[d] = main[d] + jnp.where(lane == 0, ends, 0.0)
    main = real_forward(main)
    rim = real_forward([piece[:1, :] for piece in rim])
    edge[...] = jnp.zeros_like(edge)
    left[...] = jnp.zeros_like(left)
    for h in range(2):
        edge[h, :rows, :] = main[h]
        edge[h, rows : rows + 1, :] = rim[h]
    for a in range(1, half):
        c, s = table.turn(a)
        for first, count, (re, im) in (
            (a, rows, (main[a + 1], main[half + a])),
            (rows * half + a, 1, (rim[a + 1], rim[half + a])),
        ):
            left[0, pl.ds(first, count, stride=half), :] = re * c + im * s
            left[1, pl.ds(first, count, stride=half), :] = im * c - re * s
    inner = product(jnp.concatenate([left[0], left[1]], axis=1), table.inner(3))
    for h in range(2):
        modes_ref[h, :, :] = inner[: (rows + 1) * half, h * lanes : (h + 1) * lanes]
        outer = product(edge[h], table.outer(h, 3))
        modes_ref[h, pl.ds(0, rows, stride=half), :] = outer[:rows]
        modes_ref[h, rows * half : rows * half + 1, :] = outer[rows : rows + 1]
    spectrum = row_list(modes_ref, rows, half)
    line = Line(table.decay(), rows, parts_y)
    below = line.low[0] * spectrum[0]
    above = line.high[rows] * spectrum[rows]
    for i in range(1, rows + 1):
        below = line.low[i] * spectrum[i] + line.step * below
        above = line.high[rows - i] * spectrum[rows - i] + line.step * above
    for other in range(send_ref.shape[0]):
        send_ref[other, :half, :] = below
        send_ref[other, half:, :] = above


def row_list(modes_ref, rows, half):
    return [
        jnp.concatenate([modes_ref[h, i * half : (i + 1) * half, :] for h in range(2)], axis=1)
        for i in range(rows + 1)
    ]


def near_kernel(rows, near, in_ref, table_ref, mine_ref, send_ref):
    half = in_ref.shape[1] // 2
    step = jnp.exp(-rows * table_ref[:half, :])
    place, group = lax.rem(lax.axis_index("gy"), near), lax.div(lax.axis_index("gy"), near)
    below = above = jnp.zeros_like(step)
    for i in range(near):
        j = near - 1 - i
        mine_ref[:half, :] = jnp.where(place == i, below, mine_ref[:half, :]) if i else below
        mine_ref[half:, :] = jnp.where(place == j, above, mine_ref[half:, :]) if i else above
        below = in_ref[i, :half, :] + step * below
        above = in_ref[j, half:, :] + step * above
    for other in range(send_ref.shape[0]):
        send_ref[other, :, :] = jnp.where(group < other, below, above)


def entering(pieces_ref, mine, step):
    count = pieces_ref.shape[0]
    below = above = jnp.zeros_like(step)
    for i in range(count):
        j = count - 1 - i
        below = jnp.where(i < mine, pieces_ref[i] + step * below, below)
        above = jnp.where(j > mine, pieces_ref[j] + step * above, above)
    return below, above


def solve_kernel(rows, parts_y, near, in_ref, mine_ref, modes_ref, matrix_ref, table_ref, out_ref, left, edge):
    blocks, _, _, lanes = out_ref.shape
    half = blocks // 2
    table = Tables(matrix_ref, table_ref, lanes, half)
    row, lane = places((rows, lanes))
    decay = table.decay()
    place, group = lax.rem(lax.axis_index("gy"), near), lax.div(lax.axis_index("gy"), near)
    far_below, far_above = entering(in_ref, group, jnp.exp(-(rows * near) * decay))
    ahead = (rows * place).astype(jnp.float32)
    below = mine_ref[:half, :] + jnp.exp(-decay * ahead) * far_below
    above = mine_ref[half:, :] + jnp.exp(-decay * (rows * (near - 1) - ahead)) * far_above
    line = Line(decay, rows, parts_y)
    spectrum = row_list(modes_ref, rows, half)
    gain = line.gain()
    from_below = [line.low[0] * spectrum[0] + below]
    for i in range(1, rows + 1):
        from_below.append(line.low[i] * spectrum[i] + line.step * from_below[-1])
    from_above = above
    edge[...] = jnp.zeros_like(edge)
    for i in reversed(range(rows + 1)):
        solved = gain * (line.high[i] * from_below[i] + line.low[i] * from_above)
        for h, sign in ((0, 1.0), (1, -1.0)):
            part = solved[:, h * lanes : (h + 1) * lanes]
            edge[h, i : i + 1, :] = part[:1, :]
            left[h, i * half : (i + 1) * half, :] = sign * part
        from_above = line.step * (from_above + line.high[i] * spectrum[i])
    left[:, (rows + 1) * half :, :] = jnp.zeros_like(left[:, (rows + 1) * half :, :])
    inner = product(jnp.concatenate([left[0], left[1]], axis=1), table.inner(3))
    main, rim = [], []
    for h in range(2):
        left[h, :, :] = inner[:, h * lanes : (h + 1) * lanes]
        outer = product(edge[h], table.outer(h, 3), transposed=True)
        main.append(outer[:rows])
        rim.append(outer[rows : rows + 1])
    main, rim = main + [None] * (blocks - 2), rim + [None] * (blocks - 2)
    for a in range(1, half):
        c, s = table.turn(a)
        for planes, first, count in ((main, a, rows), (rim, rows * half + a, 1)):
            re = left[0, pl.ds(first, count, stride=half), :]
            im = left[1, pl.ds(first, count, stride=half), :]
            planes[a + 1] = re * c + im * s
            planes[half + a] = re * s - im * c
    main, rim = real_inverse(main), real_inverse(rim)
    for d in range(blocks):
        ends = column_to_row(main[(d + 1) % blocks][:, :1], row, lane)
        put(out_ref, d, main[d], jnp.where(row == 0, rim[d], ends))


def correct_kernel(
    parts_y, in_ref, stream_ref, normal_ref, span_ref, pressure_ref, stream_out, normal_out, span_out, held
):
    planes, _, _, cells = in_ref.shape
    rows = stream_ref.shape[0] // planes
    row, lane = places((rows, cells))
    keep = wall_keep(row, rows - 1, parts_y)
    pressure, rim = take(in_ref, held)
    pressure, rim = real_inverse(pressure), real_inverse(rim)
    for z in range(planes):
        here = pl.ds(z, rows, stride=planes)
        p = pressure[z]
        upper = jnp.where(row == rows - 1, rim[z][:1, :], pltpu.roll(p, rows - 1, 0))
        right = jnp.where(lane == cells - 1, row_to_column(rim[z][1:2, :], row, lane), pltpu.roll(p, cells - 1, 1))
        pressure_ref[here, :] = p
        stream_out[here, :] = stream_ref[here, :] - grid_ratio * (right - p)
        normal_out[here, :] = (normal_ref[here, :] - (upper - p)) * keep
        span_out[here, :] = span_ref[here, :] - grid_ratio * (pressure[(z + 1) % planes] - p)


def shape_of(*dims):
    return jax.ShapeDtypeStruct(dims, jnp.float32)


def per_device(stream_vel, normal_vel, span_vel):
    rows, planes, cells = stream_vel.shape
    parts_x, parts_y = lax.axis_size("gx"), lax.axis_size("gy")
    blocks, half = parts_x, parts_x // 2
    near = 1 << (parts_y.bit_length() // 2)
    far = parts_y // near
    if planes != parts_x or rows != half or near * far != parts_y:
        raise ValueError("unsupported sizes")
    matrices, table = tables(planes, cells, blocks, cells * parts_x)
    near_groups = [[i * near + k for k in range(near)] for i in range(far)]
    far_groups = [[i + k * near for k in range(far)] for i in range(near)]
    flat = [a.reshape(rows * planes, cells) for a in (stream_vel, normal_vel, span_vel)]
    message = shape_of(blocks, rows // 2 + 1, 2, cells)
    held = pltpu.VMEM((blocks, rows, cells), jnp.float32)
    room = pltpu.CompilerParams(vmem_limit_bytes=8 << 20)
    scratch = [
        pltpu.VMEM((2, (rows + 2) * half, cells), jnp.float32),
        pltpu.VMEM((2, 2 * rows, cells), jnp.float32),
    ]

    kept = [matrices, *flat]
    sent, local, *kept = pl.pallas_call(
        functools.partial(source_kernel, planes, parts_y),
        out_shape=(message, shape_of(2 * half, 2 * cells), *(jax.ShapeDtypeStruct(a.shape, a.dtype) for a in kept)),
        in_specs=[pl.BlockSpec(memory_space=pltpu.HBM)] * 5,
        scratch_shapes=[pltpu.SemaphoreType.DMA((6,))],
        compiler_params=room,
        name="source",
    )(*(pltpu.with_memory_space_constraint(a, pltpu.HBM) for a in (*flat, table, matrices)))
    matrices, *flat = kept
    taken = lax.all_to_all(sent, "gx", 0, 0)
    sent, modes = pl.pallas_call(
        functools.partial(modes_kernel, rows, parts_y),
        out_shape=(shape_of(near, 2 * half, 2 * cells), shape_of(2, (rows + 1) * half, cells)),
        scratch_shapes=[*scratch, held],
        compiler_params=room,
        name="modes",
    )(taken, matrices, local)
    taken = lax.all_to_all(sent, "gy", 0, 0, axis_index_groups=near_groups)
    mine, sent = pl.pallas_call(
        functools.partial(near_kernel, rows, near),
        out_shape=(shape_of(2 * half, 2 * cells), shape_of(far, half, 2 * cells)),
        compiler_params=room,
        name="near",
    )(taken, local)
    taken = lax.all_to_all(sent, "gy", 0, 0, axis_index_groups=far_groups)
    sent = pl.pallas_call(
        functools.partial(solve_kernel, rows, parts_y, near),
        out_shape=message,
        scratch_shapes=scratch,
        compiler_params=room,
        name="solve",
    )(taken, mine, modes, matrices, local)
    taken = lax.all_to_all(sent, "gx", 0, 0)
    outs = pl.pallas_call(
        functools.partial(correct_kernel, parts_y),
        out_shape=(shape_of(rows * planes, cells),) * 4,
        scratch_shapes=[held],
        compiler_params=room,
        name="correct",
    )(taken, *flat)
    return tuple(a.reshape(rows, planes, cells) for a in outs)


def solution(mesh):
    spec = P("gy", None, "gx")
    return jax.shard_map(
        per_device, mesh=mesh, in_specs=(spec,) * 3, out_specs=(spec,) * 4, check_vma=False
    )
```

```python
import functools
import math

import jax
import jax.numpy as jnp
import numpy as np
from jax import lax
from jax.experimental import pallas as pl
from jax.experimental.pallas import tpu as pltpu
from jax.sharding import PartitionSpec as P

shift_term = 1.0 / 1024.0
grid_ratio = 1.0 / 128.0


def weighted(terms):
    total = None
    for factor, value in terms:
        if abs(factor) < 1e-12:
            continue
        term = value * factor
        total = term if total is None else total + term
    return total


def angle_tables(count):
    half = count // 2
    cosine = [[math.cos(2 * math.pi * (k * i % count) / count) for i in range(count)] for k in range(half + 1)]
    sine = [[math.sin(2 * math.pi * (k * i % count) / count) for i in range(count)] for k in range(half + 1)]
    return cosine, sine


def real_forward(values):
    count = len(values)
    half = count // 2
    cosine, sine = angle_tables(count)
    even = [values[0]] + [values[i] + values[count - i] for i in range(1, half)] + [values[half]]
    odd = [None] + [values[i] - values[count - i] for i in range(1, half)]
    edge, inner = 1 / math.sqrt(count), math.sqrt(2 / count)
    first = weighted([(edge, value) for value in even])
    middle = weighted([(edge * (-1) ** i, value) for i, value in enumerate(even)])
    cosines = [weighted([(inner * cosine[k][i], even[i]) for i in range(half + 1)]) for k in range(1, half)]
    sines = [weighted([(-inner * sine[k][i], odd[i]) for i in range(1, half)]) for k in range(1, half)]
    return [first, middle, *cosines, *sines]


def real_inverse(planes):
    count = len(planes)
    half = count // 2
    cosine, sine = angle_tables(count)
    edge, inner = 1 / math.sqrt(count), math.sqrt(2 / count)
    values = [None] * count
    for i in range(half + 1):
        even = weighted(
            [(edge, planes[0]), (edge * (-1) ** i, planes[1])]
            + [(inner * cosine[k][i], planes[k + 1]) for k in range(1, half)]
        )
        if i in (0, half):
            values[i] = even
            continue
        odd = weighted([(-inner * sine[k][i], planes[half + k]) for k in range(1, half)])
        values[i] = even + odd
        values[count - i] = even - odd
    return values


def plane_modes(count):
    half = count // 2
    return np.array([0, half, *range(1, half), *range(1, half)])


def tables(planes, lanes, blocks, length_x):
    half = blocks // 2
    t = np.arange(lanes)
    phases = np.arange(half)
    turn = 2 * np.pi * phases[:, None] * t[None, :] / length_x
    turns = np.concatenate([np.cos(turn), np.sin(turn)])
    product = 2 * np.pi * (t[:, None] * t[None, :] % lanes) / lanes
    scale = 1 / math.sqrt(lanes)
    c, s = np.cos(product) * scale, np.sin(product) * scale
    inner = np.block([[c, -s], [s, c]])
    root = math.sqrt(2.0)
    n = lanes // 2
    first = np.concatenate([c[:, :1], root * c[:, 1:n], c[:, n : n + 1], -root * s[:, 1:n]], axis=1)
    shifted = np.pi * (t[:, None] * (2 * np.arange(n)[None, :] + 1) % (2 * lanes)) / lanes
    middle = root * scale * np.concatenate([np.cos(shifted), -np.sin(shifted)], axis=1)
    outer = np.concatenate([first, middle], axis=1)
    mode_x = np.zeros((half, 2 * lanes))
    mode_x[1:] = phases[1:, None] + blocks * np.concatenate([t, t])[None, :]
    mode_x[0, : n + 1] = blocks * np.arange(n + 1)
    mode_x[0, n + 1 : lanes] = blocks * np.arange(1, n)
    mode_x[0, lanes:] = half + blocks * np.concatenate([np.arange(n), np.arange(n)])
    wave_x = (2 * np.sin(np.pi * mode_x / length_x)) ** 2
    wave_z = (2 * np.sin(np.pi * plane_modes(planes) / planes)) ** 2
    eigen_sum = grid_ratio * grid_ratio * (wave_z[:, None, None] + wave_x[None]) + shift_term
    decay = 2 * np.arcsinh(np.sqrt(eigen_sum) / 2)
    decay = decay.reshape(planes * half, 2 * lanes)
    turns = np.concatenate([turns[:half], turns[half:]], axis=1)
    matrices = np.concatenate([inner, outer])
    return jnp.asarray(matrices, jnp.float32), jnp.asarray(np.concatenate([decay, turns]), jnp.float32)


def split(values, count):
    parts = []
    for _ in range(count):
        parts.append(values.astype(jnp.bfloat16))
        values = values - parts[-1].astype(jnp.float32)
    return parts


def product(values, matrix, transposed=False):
    parts, matrix, rows = split(values, 3), split(matrix, 3), values.shape[0]
    dims = (((1,), (1 if transposed else 0,)), ((), ()))
    terms = []
    for j, piece in enumerate(matrix):
        stacked = parts[: len(parts) - j]
        stacked = jnp.concatenate(stacked) if len(stacked) > 1 else stacked[0]
        terms.append(lax.dot_general(stacked, piece, dims, preferred_element_type=jnp.float32))
    total = None
    for size in reversed(range(len(matrix))):
        for j in range(size + 1):
            i = size - j
            term = terms[j][i * rows : (i + 1) * rows]
            total = term if total is None else total + term
    return total


class Tables:
    def __init__(self, matrix_ref, ref, lanes, half):
        self.matrix_ref, self.ref, self.lanes, self.half = matrix_ref, ref, lanes, half

    def inner(self):
        return self.matrix_ref[: 2 * self.lanes, :]

    def outer(self, h):
        return self.matrix_ref[2 * self.lanes :, h * self.lanes : (h + 1) * self.lanes]

    def decay(self):
        return self.ref[: self.half, :]

    def turn(self, a):
        line = self.half + a
        return self.ref[line : line + 1, : self.lanes], self.ref[line : line + 1, self.lanes :]


def places(shape):
    return lax.broadcasted_iota(jnp.int32, shape, 0), lax.broadcasted_iota(jnp.int32, shape, 1)


def column_to_row(column, row, lane):
    return jnp.sum(jnp.where(row == lane, column, 0.0), axis=0, keepdims=True)


def row_to_column(line, row, lane):
    return jnp.sum(jnp.where(row == lane, line, 0.0), axis=1, keepdims=True)


def wall_keep(row, last_row, parts_y):
    is_wall = jnp.logical_and(row == last_row, lax.axis_index("gy") == parts_y - 1)
    return jnp.where(is_wall, 0.0, 1.0)


def source_kernel(
    planes,
    parts_y,
    stream_hbm,
    normal_hbm,
    span_hbm,
    table_hbm,
    matrix_hbm,
    out_ref,
    local_ref,
    matrix_ref,
    stream_ref,
    normal_ref,
    span_ref,
    done,
):
    half = local_ref.shape[0] // 2
    decay_rows = pl.ds(pl.multiple_of(lax.axis_index("gx") * half, half), half)
    turn_rows = pl.ds(table_hbm.shape[0] - half, half)
    copies = [
        pltpu.make_async_copy(stream_hbm, stream_ref, done.at[0]),
        pltpu.make_async_copy(normal_hbm, normal_ref, done.at[1]),
        pltpu.make_async_copy(span_hbm, span_ref, done.at[2]),
        pltpu.make_async_copy(table_hbm.at[decay_rows, :], local_ref.at[:half, :], done.at[3]),
        pltpu.make_async_copy(table_hbm.at[turn_rows, :], local_ref.at[half:, :], done.at[4]),
        pltpu.make_async_copy(matrix_hbm, matrix_ref, done.at[5]),
    ]
    for copy in copies:
        copy.start()
    for copy in copies[:3]:
        copy.wait()
    cells = stream_ref.shape[1]
    rows = stream_ref.shape[0] // planes
    row, lane = places((rows, cells))
    keep = wall_keep(row, rows - 1, parts_y)

    def plane(ref, z):
        return ref[pl.ds(z, rows, stride=planes), :]

    main, rim = [], []
    span_before = plane(span_ref, planes - 1)
    for z in range(planes):
        stream, normal, span = plane(stream_ref, z), plane(normal_ref, z) * keep, plane(span_ref, z)
        stream_left = jnp.where(lane == 0, 0.0, pltpu.roll(stream, 1, 1))
        normal_turned = pltpu.roll(normal, 1, 0)
        normal_below = jnp.where(row == 0, 0.0, normal_turned)
        main.append(
            grid_ratio * (stream - stream_left) + (normal - normal_below) + grid_ratio * (span - span_before)
        )
        ends = column_to_row(stream[:, cells - 1 :], row, lane)
        rim.append(jnp.where(row == 0, -normal_turned, jnp.where(row == 1, -grid_ratio * ends, 0.0)))
        span_before = span
    main, rim = real_forward(main), real_forward(rim)
    for k in range(planes):
        put(out_ref, k, main[k], rim[k])
    for copy in copies[3:]:
        copy.wait()


def put(ref, index, main, rim):
    pairs = ref.shape[1] - 1
    for j in range(pairs):
        ref[index, j] = main[2 * j : 2 * j + 2, :]
    ref[index, pairs] = rim[:2, :]


def take(ref, held):
    count, pairs = ref.shape[0], ref.shape[1] - 1
    for i in range(count):
        for j in range(pairs):
            held[i, 2 * j : 2 * j + 2, :] = ref[i, j]
    return [held[i] for i in range(count)], [ref[i, pairs] for i in range(count)]


class Line:
    def __init__(self, decay, rows, parts_y):
        base = (lax.axis_index("gy") * rows).astype(jnp.float32)
        total = rows * parts_y
        self.step = jnp.exp(-decay)
        square, grown = self.step * self.step, jnp.exp(2.0 * decay)
        low = jnp.exp(-decay * (2.0 * base + 1.0))
        high = jnp.exp(-decay * (2.0 * (total - base) - 1.0))
        self.low, self.high = [], []
        for _ in range(rows + 1):
            self.low.append(1.0 + low)
            self.high.append(1.0 + high)
            low, high = low * square, high * grown
        self.decay, self.total = decay, total

    def gain(self):
        return -1.0 / ((jnp.exp(self.decay) - self.step) * (1.0 - jnp.exp(self.decay * (-2.0 * self.total))))


def modes_kernel(rows, parts_y, in_ref, matrix_ref, table_ref, send_ref, modes_ref, left, edge, held):
    blocks, _, _, lanes = in_ref.shape
    half = blocks // 2
    table = Tables(matrix_ref, table_ref, lanes, half)
    row, lane = places((rows, lanes))
    main, rim = take(in_ref, held)
    for d in range(blocks):
        ends = row_to_column(rim[d - 1][1:2, :], row, lane)
        main[d] = main[d] + jnp.where(lane == 0, ends, 0.0)
    main = real_forward(main)
    rim = real_forward([piece[:1, :] for piece in rim])
    edge[...] = jnp.zeros_like(edge)
    left[...] = jnp.zeros_like(left)
    for h in range(2):
        edge[h, :rows, :] = main[h]
        edge[h, rows : rows + 1, :] = rim[h]
    for a in range(1, half):
        c, s = table.turn(a)
        for first, count, (re, im) in (
            (a, rows, (main[a + 1], main[half + a])),
            (rows * half + a, 1, (rim[a + 1], rim[half + a])),
        ):
            left[0, pl.ds(first, count, stride=half), :] = re * c + im * s
            left[1, pl.ds(first, count, stride=half), :] = im * c - re * s
    inner = product(jnp.concatenate([left[0], left[1]], axis=1), table.inner())
    for h in range(2):
        modes_ref[h, :, :] = inner[: (rows + 1) * half, h * lanes : (h + 1) * lanes]
        outer = product(edge[h], table.outer(h))
        modes_ref[h, pl.ds(0, rows, stride=half), :] = outer[:rows]
        modes_ref[h, rows * half : rows * half + 1, :] = outer[rows : rows + 1]
    spectrum = row_list(modes_ref, rows, half)
    line = Line(table.decay(), rows, parts_y)
    below = line.low[0] * spectrum[0]
    above = line.high[rows] * spectrum[rows]
    for i in range(1, rows + 1):
        below = line.low[i] * spectrum[i] + line.step * below
        above = line.high[rows - i] * spectrum[rows - i] + line.step * above
    for other in range(send_ref.shape[0]):
        send_ref[other, :half, :] = below
        send_ref[other, half:, :] = above


def row_list(modes_ref, rows, half):
    return [
        jnp.concatenate([modes_ref[h, i * half : (i + 1) * half, :] for h in range(2)], axis=1)
        for i in range(rows + 1)
    ]


def near_kernel(rows, near, in_ref, table_ref, mine_ref, send_ref):
    half = in_ref.shape[1] // 2
    step = jnp.exp(-rows * table_ref[:half, :])
    place, group = lax.rem(lax.axis_index("gy"), near), lax.div(lax.axis_index("gy"), near)
    below = above = jnp.zeros_like(step)
    for i in range(near):
        j = near - 1 - i
        mine_ref[:half, :] = jnp.where(place == i, below, mine_ref[:half, :]) if i else below
        mine_ref[half:, :] = jnp.where(place == j, above, mine_ref[half:, :]) if i else above
        below = in_ref[i, :half, :] + step * below
        above = in_ref[j, half:, :] + step * above
    for other in range(send_ref.shape[0]):
        send_ref[other, :, :] = jnp.where(group < other, below, above)


def entering(pieces_ref, mine, step):
    count = pieces_ref.shape[0]
    below = above = jnp.zeros_like(step)
    for i in range(count):
        j = count - 1 - i
        below = jnp.where(i < mine, pieces_ref[i] + step * below, below)
        above = jnp.where(j > mine, pieces_ref[j] + step * above, above)
    return below, above


def solve_kernel(rows, parts_y, near, in_ref, mine_ref, modes_ref, matrix_ref, table_ref, out_ref, left, edge):
    blocks, _, _, lanes = out_ref.shape
    half = blocks // 2
    table = Tables(matrix_ref, table_ref, lanes, half)
    row, lane = places((rows, lanes))
    decay = table.decay()
    place, group = lax.rem(lax.axis_index("gy"), near), lax.div(lax.axis_index("gy"), near)
    far_below, far_above = entering(in_ref, group, jnp.exp(-(rows * near) * decay))
    ahead = (rows * place).astype(jnp.float32)
    below = mine_ref[:half, :] + jnp.exp(-decay * ahead) * far_below
    above = mine_ref[half:, :] + jnp.exp(-decay * (rows * (near - 1) - ahead)) * far_above
    line = Line(decay, rows, parts_y)
    spectrum = row_list(modes_ref, rows, half)
    gain = line.gain()
    from_below = [line.low[0] * spectrum[0] + below]
    for i in range(1, rows + 1):
        from_below.append(line.low[i] * spectrum[i] + line.step * from_below[-1])
    from_above = above
    edge[...] = jnp.zeros_like(edge)
    for i in reversed(range(rows + 1)):
        solved = gain * (line.high[i] * from_below[i] + line.low[i] * from_above)
        for h, sign in ((0, 1.0), (1, -1.0)):
            part = solved[:, h * lanes : (h + 1) * lanes]
            edge[h, i : i + 1, :] = part[:1, :]
            left[h, i * half : (i + 1) * half, :] = sign * part
        from_above = line.step * (from_above + line.high[i] * spectrum[i])
    left[:, (rows + 1) * half :, :] = jnp.zeros_like(left[:, (rows + 1) * half :, :])
    inner = product(jnp.concatenate([left[0], left[1]], axis=1), table.inner())
    main, rim = [], []
    for h in range(2):
        left[h, :, :] = inner[:, h * lanes : (h + 1) * lanes]
        outer = product(edge[h], table.outer(h), transposed=True)
        main.append(outer[:rows])
        rim.append(outer[rows : rows + 1])
    main, rim = main + [None] * (blocks - 2), rim + [None] * (blocks - 2)
    for a in range(1, half):
        c, s = table.turn(a)
        for planes, first, count in ((main, a, rows), (rim, rows * half + a, 1)):
            re = left[0, pl.ds(first, count, stride=half), :]
            im = left[1, pl.ds(first, count, stride=half), :]
            planes[a + 1] = re * c + im * s
            planes[half + a] = re * s - im * c
    main, rim = real_inverse(main), real_inverse(rim)
    for d in range(blocks):
        ends = column_to_row(main[(d + 1) % blocks][:, :1], row, lane)
        put(out_ref, d, main[d], jnp.where(row == 0, rim[d], ends))


def correct_kernel(
    parts_y, in_ref, stream_ref, normal_ref, span_ref, pressure_ref, stream_out, normal_out, span_out, held
):
    planes, _, _, cells = in_ref.shape
    rows = stream_ref.shape[0] // planes
    row, lane = places((rows, cells))
    keep = wall_keep(row, rows - 1, parts_y)
    pressure, rim = take(in_ref, held)
    pressure, rim = real_inverse(pressure), real_inverse(rim)
    for z in range(planes):
        here = pl.ds(z, rows, stride=planes)
        p = pressure[z]
        upper = jnp.where(row == rows - 1, rim[z][:1, :], pltpu.roll(p, rows - 1, 0))
        right = jnp.where(lane == cells - 1, row_to_column(rim[z][1:2, :], row, lane), pltpu.roll(p, cells - 1, 1))
        pressure_ref[here, :] = p
        stream_out[here, :] = stream_ref[here, :] - grid_ratio * (right - p)
        normal_out[here, :] = (normal_ref[here, :] - (upper - p)) * keep
        span_out[here, :] = span_ref[here, :] - grid_ratio * (pressure[(z + 1) % planes] - p)


def shape_of(*dims):
    return jax.ShapeDtypeStruct(dims, jnp.float32)


def per_device(stream_vel, normal_vel, span_vel):
    rows, planes, cells = stream_vel.shape
    parts_x, parts_y = lax.axis_size("gx"), lax.axis_size("gy")
    blocks, half = parts_x, parts_x // 2
    near = 1 << (parts_y.bit_length() // 2)
    far = parts_y // near
    if planes != parts_x or rows != half or near * far != parts_y:
        raise ValueError("unsupported sizes")
    matrices, table = tables(planes, cells, blocks, cells * parts_x)
    near_groups = [[i * near + k for k in range(near)] for i in range(far)]
    far_groups = [[i + k * near for k in range(far)] for i in range(near)]
    flat = [a.reshape(rows * planes, cells) for a in (stream_vel, normal_vel, span_vel)]
    message = shape_of(blocks, rows // 2 + 1, 2, cells)
    held = pltpu.VMEM((blocks, rows, cells), jnp.float32)
    room = pltpu.CompilerParams(vmem_limit_bytes=8 << 20)
    scratch = [
        pltpu.VMEM((2, (rows + 2) * half, cells), jnp.float32),
        pltpu.VMEM((2, 2 * rows, cells), jnp.float32),
    ]

    kept = [matrices, *flat]
    sent, local, *kept = pl.pallas_call(
        functools.partial(source_kernel, planes, parts_y),
        out_shape=(message, shape_of(2 * half, 2 * cells), *(jax.ShapeDtypeStruct(a.shape, a.dtype) for a in kept)),
        in_specs=[pl.BlockSpec(memory_space=pltpu.HBM)] * 5,
        scratch_shapes=[pltpu.SemaphoreType.DMA((6,))],
        compiler_params=room,
        name="source",
    )(*(pltpu.with_memory_space_constraint(a, pltpu.HBM) for a in (*flat, table, matrices)))
    matrices, *flat = kept
    taken = lax.all_to_all(sent, "gx", 0, 0)
    sent, modes = pl.pallas_call(
        functools.partial(modes_kernel, rows, parts_y),
        out_shape=(shape_of(near, 2 * half, 2 * cells), shape_of(2, (rows + 1) * half, cells)),
        scratch_shapes=[*scratch, held],
        compiler_params=room,
        name="modes",
    )(taken, matrices, local)
    taken = lax.all_to_all(sent, "gy", 0, 0, axis_index_groups=near_groups)
    mine, sent = pl.pallas_call(
        functools.partial(near_kernel, rows, near),
        out_shape=(shape_of(2 * half, 2 * cells), shape_of(far, half, 2 * cells)),
        compiler_params=room,
        name="near",
    )(taken, local)
    taken = lax.all_to_all(sent, "gy", 0, 0, axis_index_groups=far_groups)
    sent = pl.pallas_call(
        functools.partial(solve_kernel, rows, parts_y, near),
        out_shape=message,
        scratch_shapes=scratch,
        compiler_params=room,
        name="solve",
    )(taken, mine, modes, matrices, local)
    taken = lax.all_to_all(sent, "gx", 0, 0)
    outs = pl.pallas_call(
        functools.partial(correct_kernel, parts_y),
        out_shape=(shape_of(rows * planes, cells),) * 4,
        scratch_shapes=[held],
        compiler_params=room,
        name="correct",
    )(taken, *flat)
    return tuple(a.reshape(rows, planes, cells) for a in outs)


def solution(mesh):
    spec = P("gy", None, "gx")
    return jax.shard_map(
        per_device, mesh=mesh, in_specs=(spec,) * 3, out_specs=(spec,) * 4, check_vma=False
    )
```

```python
import functools
import math

import jax
import jax.numpy as jnp
import numpy as np
from jax import lax
from jax.experimental import pallas as pl
from jax.experimental.pallas import tpu as pltpu
from jax.sharding import PartitionSpec as P

shift_term = 1.0 / 1024.0
grid_ratio = 1.0 / 128.0


def weighted(terms):
    total = None
    for factor, value in terms:
        if abs(factor) < 1e-12:
            continue
        term = value * factor
        total = term if total is None else total + term
    return total


def angle_tables(count):
    half = count // 2
    cosine = [[math.cos(2 * math.pi * (k * i % count) / count) for i in range(count)] for k in range(half + 1)]
    sine = [[math.sin(2 * math.pi * (k * i % count) / count) for i in range(count)] for k in range(half + 1)]
    return cosine, sine


def real_forward(values):
    count = len(values)
    half = count // 2
    cosine, sine = angle_tables(count)
    even = [values[0]] + [values[i] + values[count - i] for i in range(1, half)] + [values[half]]
    odd = [None] + [values[i] - values[count - i] for i in range(1, half)]
    edge, inner = 1 / math.sqrt(count), math.sqrt(2 / count)
    first = weighted([(edge, value) for value in even])
    middle = weighted([(edge * (-1) ** i, value) for i, value in enumerate(even)])
    cosines = [weighted([(inner * cosine[k][i], even[i]) for i in range(half + 1)]) for k in range(1, half)]
    sines = [weighted([(-inner * sine[k][i], odd[i]) for i in range(1, half)]) for k in range(1, half)]
    return [first, middle, *cosines, *sines]


def real_inverse(planes):
    count = len(planes)
    half = count // 2
    cosine, sine = angle_tables(count)
    edge, inner = 1 / math.sqrt(count), math.sqrt(2 / count)
    values = [None] * count
    for i in range(half + 1):
        even = weighted(
            [(edge, planes[0]), (edge * (-1) ** i, planes[1])]
            + [(inner * cosine[k][i], planes[k + 1]) for k in range(1, half)]
        )
        if i in (0, half):
            values[i] = even
            continue
        odd = weighted([(-inner * sine[k][i], planes[half + k]) for k in range(1, half)])
        values[i] = even + odd
        values[count - i] = even - odd
    return values


def halves_apart(count):
    order = [i // 2 + i % 2 * (count // 2) for i in range(count)]
    return order, [order.index(i) for i in range(count)]


def evens_first(count):
    order = [*range(0, count, 2), *range(1, count, 2)]
    return order, [order.index(i) for i in range(count)]


def plane_modes(count):
    half = count // 2
    return np.array([0, half, *range(1, half), *range(1, half)])


def tables(planes, lanes, blocks, length_x):
    half = blocks // 2
    t = np.arange(lanes)
    phases = np.arange(half)
    turn = 2 * np.pi * phases[:, None] * t[None, :] / length_x
    turns = np.concatenate([np.cos(turn), np.sin(turn)])
    product = 2 * np.pi * (t[:, None] * t[None, :] % lanes) / lanes
    scale = 1 / math.sqrt(lanes)
    c, s = np.cos(product) * scale, np.sin(product) * scale
    inner = np.block([[c, -s], [s, c]])
    root = math.sqrt(2.0)
    n = lanes // 2
    first = np.concatenate([c[:, :1], root * c[:, 1:n], c[:, n : n + 1], -root * s[:, 1:n]], axis=1)
    shifted = np.pi * (t[:, None] * (2 * np.arange(n)[None, :] + 1) % (2 * lanes)) / lanes
    middle = root * scale * np.concatenate([np.cos(shifted), -np.sin(shifted)], axis=1)
    outer = np.concatenate([first, middle], axis=1)
    mode_x = np.zeros((half, 2 * lanes))
    mode_x[1:] = phases[1:, None] + blocks * np.concatenate([t, t])[None, :]
    mode_x[0, : n + 1] = blocks * np.arange(n + 1)
    mode_x[0, n + 1 : lanes] = blocks * np.arange(1, n)
    mode_x[0, lanes:] = half + blocks * np.concatenate([np.arange(n), np.arange(n)])
    wave_x = (2 * np.sin(np.pi * mode_x / length_x)) ** 2
    wave_z = (2 * np.sin(np.pi * plane_modes(planes) / planes)) ** 2
    eigen_sum = grid_ratio * grid_ratio * (wave_z[:, None, None] + wave_x[None]) + shift_term
    decay = 2 * np.arcsinh(np.sqrt(eigen_sum) / 2)
    decay = decay.reshape(planes * half, 2 * lanes)
    turns = np.concatenate([turns[:half], turns[half:]], axis=1)
    matrices = np.concatenate([inner, outer])
    return jnp.asarray(matrices, jnp.float32), jnp.asarray(np.concatenate([decay, turns]), jnp.float32)


def split(values, count):
    parts = []
    for _ in range(count):
        parts.append(values.astype(jnp.bfloat16))
        values = values - parts[-1].astype(jnp.float32)
    return parts


def product(values, matrix, transposed=False):
    parts, matrix, rows = split(values, 3), split(matrix, 3), values.shape[0]
    dims = (((1,), (1 if transposed else 0,)), ((), ()))
    terms = []
    for j, piece in enumerate(matrix):
        stacked = parts[: len(parts) - j]
        stacked = jnp.concatenate(stacked) if len(stacked) > 1 else stacked[0]
        terms.append(lax.dot_general(stacked, piece, dims, preferred_element_type=jnp.float32))
    total = None
    for size in reversed(range(len(matrix))):
        for j in range(size + 1):
            i = size - j
            term = terms[j][i * rows : (i + 1) * rows]
            total = term if total is None else total + term
    return total


class Tables:
    def __init__(self, matrix_ref, ref, lanes, half):
        self.matrix_ref, self.ref, self.lanes, self.half = matrix_ref, ref, lanes, half

    def inner(self):
        return self.matrix_ref[: 2 * self.lanes, :]

    def outer(self, h):
        return self.matrix_ref[2 * self.lanes :, h * self.lanes : (h + 1) * self.lanes]

    def decay(self):
        return self.ref[: self.half, :]

    def turn(self, a):
        line = self.half + a
        return self.ref[line : line + 1, : self.lanes], self.ref[line : line + 1, self.lanes :]


def places(shape):
    return lax.broadcasted_iota(jnp.int32, shape, 0), lax.broadcasted_iota(jnp.int32, shape, 1)


def column_to_row(column, row, lane):
    return jnp.sum(jnp.where(row == lane, column, 0.0), axis=0, keepdims=True)


def row_to_column(line, row, lane):
    return jnp.sum(jnp.where(row == lane, line, 0.0), axis=1, keepdims=True)


def wall_keep(row, last_row, parts_y):
    is_wall = jnp.logical_and(row == last_row, lax.axis_index("gy") == parts_y - 1)
    return jnp.where(is_wall, 0.0, 1.0)


def source_kernel(
    planes,
    parts_y,
    stream_hbm,
    normal_hbm,
    span_hbm,
    table_hbm,
    matrix_hbm,
    out_ref,
    local_ref,
    matrix_ref,
    stream_ref,
    normal_ref,
    span_ref,
    done,
):
    half = local_ref.shape[0] // 2
    index = lax.axis_index("gx")
    plane_here = lax.rem(index, 2) * (planes // 2) + lax.div(index, 2)
    decay_rows = pl.ds(pl.multiple_of(plane_here * half, half), half)
    turn_rows = pl.ds(table_hbm.shape[0] - half, half)
    copies = [
        pltpu.make_async_copy(stream_hbm, stream_ref, done.at[0]),
        pltpu.make_async_copy(normal_hbm, normal_ref, done.at[1]),
        pltpu.make_async_copy(span_hbm, span_ref, done.at[2]),
        pltpu.make_async_copy(table_hbm.at[decay_rows, :], local_ref.at[:half, :], done.at[3]),
        pltpu.make_async_copy(table_hbm.at[turn_rows, :], local_ref.at[half:, :], done.at[4]),
        pltpu.make_async_copy(matrix_hbm, matrix_ref, done.at[5]),
    ]
    for copy in copies:
        copy.start()
    for copy in copies[:3]:
        copy.wait()
    cells = stream_ref.shape[1]
    rows = stream_ref.shape[0] // planes
    row, lane = places((rows, cells))
    keep = wall_keep(row, rows - 1, parts_y)

    def plane(ref, z):
        return ref[pl.ds(z, rows, stride=planes), :]

    main, rim = [], []
    span_before = plane(span_ref, planes - 1)
    for z in range(planes):
        stream, normal, span = plane(stream_ref, z), plane(normal_ref, z) * keep, plane(span_ref, z)
        stream_left = jnp.where(lane == 0, 0.0, pltpu.roll(stream, 1, 1))
        normal_turned = pltpu.roll(normal, 1, 0)
        normal_below = jnp.where(row == 0, 0.0, normal_turned)
        main.append(
            grid_ratio * (stream - stream_left) + (normal - normal_below) + grid_ratio * (span - span_before)
        )
        ends = column_to_row(stream[:, cells - 1 :], row, lane)
        rim.append(jnp.where(row == 0, -normal_turned, jnp.where(row == 1, -grid_ratio * ends, 0.0)))
        span_before = span
    main, rim = real_forward(main), real_forward(rim)
    for k in range(planes):
        put(out_ref, k, main[k], rim[k])
    for copy in copies[3:]:
        copy.wait()


def put(ref, index, main, rim):
    pairs = ref.shape[1] - 1
    for j in range(pairs):
        ref[index, j] = main[2 * j : 2 * j + 2, :]
    ref[index, pairs] = rim[:2, :]


def take(ref, held):
    count, pairs = ref.shape[0], ref.shape[1] - 1
    for i in range(count):
        for j in range(pairs):
            held[i, 2 * j : 2 * j + 2, :] = ref[i, j]
    return [held[i] for i in range(count)], [ref[i, pairs] for i in range(count)]


class Line:
    def __init__(self, decay, rows, parts_y):
        base = (lax.axis_index("gy") * rows).astype(jnp.float32)
        total = rows * parts_y
        self.step = jnp.exp(-decay)
        square, grown = self.step * self.step, jnp.exp(2.0 * decay)
        low = jnp.exp(-decay * (2.0 * base + 1.0))
        high = jnp.exp(-decay * (2.0 * (total - base) - 1.0))
        self.low, self.high = [], []
        for _ in range(rows + 1):
            self.low.append(1.0 + low)
            self.high.append(1.0 + high)
            low, high = low * square, high * grown
        self.decay, self.total = decay, total

    def gain(self):
        return -1.0 / ((jnp.exp(self.decay) - self.step) * (1.0 - jnp.exp(self.decay * (-2.0 * self.total))))


def modes_kernel(rows, parts_y, in_ref, matrix_ref, table_ref, send_ref, modes_ref, left, edge, held):
    blocks, _, _, lanes = in_ref.shape
    half = blocks // 2
    table = Tables(matrix_ref, table_ref, lanes, half)
    row, lane = places((rows, lanes))
    main, rim = take(in_ref, held)
    spot = evens_first(blocks)[1]
    main, rim = [main[spot[d]] for d in range(blocks)], [rim[spot[d]] for d in range(blocks)]
    for d in range(blocks):
        ends = row_to_column(rim[d - 1][1:2, :], row, lane)
        main[d] = main[d] + jnp.where(lane == 0, ends, 0.0)
    main = real_forward(main)
    rim = real_forward([piece[:1, :] for piece in rim])
    edge[...] = jnp.zeros_like(edge)
    left[...] = jnp.zeros_like(left)
    for h in range(2):
        edge[h, :rows, :] = main[h]
        edge[h, rows : rows + 1, :] = rim[h]
    for a in range(1, half):
        c, s = table.turn(a)
        for first, count, (re, im) in (
            (a, rows, (main[a + 1], main[half + a])),
            (rows * half + a, 1, (rim[a + 1], rim[half + a])),
        ):
            left[0, pl.ds(first, count, stride=half), :] = re * c + im * s
            left[1, pl.ds(first, count, stride=half), :] = im * c - re * s
    inner = product(jnp.concatenate([left[0], left[1]], axis=1), table.inner())
    for h in range(2):
        modes_ref[h, :, :] = inner[: (rows + 1) * half, h * lanes : (h + 1) * lanes]
        outer = product(edge[h], table.outer(h))
        modes_ref[h, pl.ds(0, rows, stride=half), :] = outer[:rows]
        modes_ref[h, rows * half : rows * half + 1, :] = outer[rows : rows + 1]
    spectrum = row_list(modes_ref, rows, half)
    line = Line(table.decay(), rows, parts_y)
    below = line.low[0] * spectrum[0]
    above = line.high[rows] * spectrum[rows]
    for i in range(1, rows + 1):
        below = line.low[i] * spectrum[i] + line.step * below
        above = line.high[rows - i] * spectrum[rows - i] + line.step * above
    for other in range(send_ref.shape[0]):
        send_ref[other, :half, :] = below
        send_ref[other, half:, :] = above


def row_list(modes_ref, rows, half):
    return [
        jnp.concatenate([modes_ref[h, i * half : (i + 1) * half, :] for h in range(2)], axis=1)
        for i in range(rows + 1)
    ]


def near_kernel(rows, near, in_ref, table_ref, mine_ref, send_ref):
    half = in_ref.shape[1] // 2
    step = jnp.exp(-rows * table_ref[:half, :])
    place, group = lax.rem(lax.axis_index("gy"), near), lax.div(lax.axis_index("gy"), near)
    below = above = jnp.zeros_like(step)
    spot = halves_apart(near)[1]
    for i in range(near):
        j = near - 1 - i
        mine_ref[:half, :] = jnp.where(place == i, below, mine_ref[:half, :]) if i else below
        mine_ref[half:, :] = jnp.where(place == j, above, mine_ref[half:, :]) if i else above
        below = in_ref[spot[i], :half, :] + step * below
        above = in_ref[spot[j], half:, :] + step * above
    for i, other in enumerate(halves_apart(send_ref.shape[0])[0]):
        send_ref[i, :, :] = jnp.where(group < other, below, above)


def entering(pieces_ref, mine, step):
    count = pieces_ref.shape[0]
    spot = halves_apart(count)[1]
    below = above = jnp.zeros_like(step)
    for i in range(count):
        j = count - 1 - i
        below = jnp.where(i < mine, pieces_ref[spot[i]] + step * below, below)
        above = jnp.where(j > mine, pieces_ref[spot[j]] + step * above, above)
    return below, above


def solve_kernel(rows, parts_y, near, in_ref, mine_ref, modes_ref, matrix_ref, table_ref, out_ref, left, edge):
    blocks, _, _, lanes = out_ref.shape
    half = blocks // 2
    table = Tables(matrix_ref, table_ref, lanes, half)
    row, lane = places((rows, lanes))
    decay = table.decay()
    place, group = lax.rem(lax.axis_index("gy"), near), lax.div(lax.axis_index("gy"), near)
    far_below, far_above = entering(in_ref, group, jnp.exp(-(rows * near) * decay))
    ahead = (rows * place).astype(jnp.float32)
    below = mine_ref[:half, :] + jnp.exp(-decay * ahead) * far_below
    above = mine_ref[half:, :] + jnp.exp(-decay * (rows * (near - 1) - ahead)) * far_above
    line = Line(decay, rows, parts_y)
    spectrum = row_list(modes_ref, rows, half)
    gain = line.gain()
    from_below = [line.low[0] * spectrum[0] + below]
    for i in range(1, rows + 1):
        from_below.append(line.low[i] * spectrum[i] + line.step * from_below[-1])
    from_above = above
    edge[...] = jnp.zeros_like(edge)
    for i in reversed(range(rows + 1)):
        solved = gain * (line.high[i] * from_below[i] + line.low[i] * from_above)
        for h, sign in ((0, 1.0), (1, -1.0)):
            part = solved[:, h * lanes : (h + 1) * lanes]
            edge[h, i : i + 1, :] = part[:1, :]
            left[h, i * half : (i + 1) * half, :] = sign * part
        from_above = line.step * (from_above + line.high[i] * spectrum[i])
    left[:, (rows + 1) * half :, :] = jnp.zeros_like(left[:, (rows + 1) * half :, :])
    inner = product(jnp.concatenate([left[0], left[1]], axis=1), table.inner())
    main, rim = [], []
    for h in range(2):
        left[h, :, :] = inner[:, h * lanes : (h + 1) * lanes]
        outer = product(edge[h], table.outer(h), transposed=True)
        main.append(outer[:rows])
        rim.append(outer[rows : rows + 1])
    main, rim = main + [None] * (blocks - 2), rim + [None] * (blocks - 2)
    for a in range(1, half):
        c, s = table.turn(a)
        for planes, first, count in ((main, a, rows), (rim, rows * half + a, 1)):
            re = left[0, pl.ds(first, count, stride=half), :]
            im = left[1, pl.ds(first, count, stride=half), :]
            planes[a + 1] = re * c + im * s
            planes[half + a] = re * s - im * c
    main, rim = real_inverse(main), real_inverse(rim)
    spot = evens_first(blocks)[1]
    for d in range(blocks):
        ends = column_to_row(main[(d + 1) % blocks][:, :1], row, lane)
        put(out_ref, spot[d], main[d], jnp.where(row == 0, rim[d], ends))


def correct_kernel(
    parts_y, in_ref, stream_ref, normal_ref, span_ref, pressure_ref, stream_out, normal_out, span_out, held
):
    planes, _, _, cells = in_ref.shape
    rows = stream_ref.shape[0] // planes
    row, lane = places((rows, cells))
    keep = wall_keep(row, rows - 1, parts_y)
    pressure, rim = take(in_ref, held)
    pressure, rim = real_inverse(pressure), real_inverse(rim)
    for z in range(planes):
        here = pl.ds(z, rows, stride=planes)
        p = pressure[z]
        upper = jnp.where(row == rows - 1, rim[z][:1, :], pltpu.roll(p, rows - 1, 0))
        right = jnp.where(lane == cells - 1, row_to_column(rim[z][1:2, :], row, lane), pltpu.roll(p, cells - 1, 1))
        pressure_ref[here, :] = p
        stream_out[here, :] = stream_ref[here, :] - grid_ratio * (right - p)
        normal_out[here, :] = (normal_ref[here, :] - (upper - p)) * keep
        span_out[here, :] = span_ref[here, :] - grid_ratio * (pressure[(z + 1) % planes] - p)


def shape_of(*dims):
    return jax.ShapeDtypeStruct(dims, jnp.float32)


def per_device(stream_vel, normal_vel, span_vel):
    rows, planes, cells = stream_vel.shape
    parts_x, parts_y = lax.axis_size("gx"), lax.axis_size("gy")
    blocks, half = parts_x, parts_x // 2
    near = 1 << (parts_y.bit_length() // 2)
    far = parts_y // near
    if planes != parts_x or rows != half or near * far != parts_y:
        raise ValueError("unsupported sizes")
    matrices, table = tables(planes, cells, blocks, cells * parts_x)
    near_groups = [[i * near + k for k in halves_apart(near)[0]] for i in range(far)]
    far_groups = [[i + k * near for k in halves_apart(far)[0]] for i in range(near)]
    flat = [a.reshape(rows * planes, cells) for a in (stream_vel, normal_vel, span_vel)]
    message = shape_of(blocks, rows // 2 + 1, 2, cells)
    held = pltpu.VMEM((blocks, rows, cells), jnp.float32)
    room = pltpu.CompilerParams(vmem_limit_bytes=8 << 20)
    scratch = [
        pltpu.VMEM((2, (rows + 2) * half, cells), jnp.float32),
        pltpu.VMEM((2, 2 * rows, cells), jnp.float32),
    ]

    kept = [matrices, *flat]
    sent, local, *kept = pl.pallas_call(
        functools.partial(source_kernel, planes, parts_y),
        out_shape=(message, shape_of(2 * half, 2 * cells), *(jax.ShapeDtypeStruct(a.shape, a.dtype) for a in kept)),
        in_specs=[pl.BlockSpec(memory_space=pltpu.HBM)] * 5,
        scratch_shapes=[pltpu.SemaphoreType.DMA((6,))],
        compiler_params=room,
        name="source",
    )(*(pltpu.with_memory_space_constraint(a, pltpu.HBM) for a in (*flat, table, matrices)))
    matrices, *flat = kept
    taken = lax.all_to_all(sent, "gx", 0, 0, axis_index_groups=[evens_first(blocks)[0]])
    sent, modes = pl.pallas_call(
        functools.partial(modes_kernel, rows, parts_y),
        out_shape=(shape_of(near, 2 * half, 2 * cells), shape_of(2, (rows + 1) * half, cells)),
        scratch_shapes=[*scratch, held],
        compiler_params=room,
        name="modes",
    )(taken, matrices, local)
    taken = lax.all_to_all(sent, "gy", 0, 0, axis_index_groups=near_groups)
    mine, sent = pl.pallas_call(
        functools.partial(near_kernel, rows, near),
        out_shape=(shape_of(2 * half, 2 * cells), shape_of(far, half, 2 * cells)),
        compiler_params=room,
        name="near",
    )(taken, local)
    taken = lax.all_to_all(sent, "gy", 0, 0, axis_index_groups=far_groups)
    sent = pl.pallas_call(
        functools.partial(solve_kernel, rows, parts_y, near),
        out_shape=message,
        scratch_shapes=scratch,
        compiler_params=room,
        name="solve",
    )(taken, mine, modes, matrices, local)
    taken = lax.all_to_all(sent, "gx", 0, 0, axis_index_groups=[evens_first(blocks)[0]])
    outs = pl.pallas_call(
        functools.partial(correct_kernel, parts_y),
        out_shape=(shape_of(rows * planes, cells),) * 4,
        scratch_shapes=[held],
        compiler_params=room,
        name="correct",
    )(taken, *flat)
    return tuple(a.reshape(rows, planes, cells) for a in outs)


def solution(mesh):
    spec = P("gy", None, "gx")
    return jax.shard_map(
        per_device, mesh=mesh, in_specs=(spec,) * 3, out_specs=(spec,) * 4, check_vma=False
    )
```

```python
import functools
import math

import jax
import jax.numpy as jnp
import numpy as np
from jax import lax
from jax.experimental import pallas as pl
from jax.experimental.pallas import tpu as pltpu
from jax.sharding import PartitionSpec as P

shift_term = 1.0 / 1024.0
grid_ratio = 1.0 / 128.0


def weighted(terms):
    total = None
    for factor, value in terms:
        if abs(factor) < 1e-12:
            continue
        term = value * factor
        total = term if total is None else total + term
    return total


def angle_tables(count):
    half = count // 2
    cosine = [[math.cos(2 * math.pi * (k * i % count) / count) for i in range(count)] for k in range(half + 1)]
    sine = [[math.sin(2 * math.pi * (k * i % count) / count) for i in range(count)] for k in range(half + 1)]
    return cosine, sine


def real_forward(values):
    count = len(values)
    half = count // 2
    cosine, sine = angle_tables(count)
    even = [values[0]] + [values[i] + values[count - i] for i in range(1, half)] + [values[half]]
    odd = [None] + [values[i] - values[count - i] for i in range(1, half)]
    edge, inner = 1 / math.sqrt(count), math.sqrt(2 / count)
    first = weighted([(edge, value) for value in even])
    middle = weighted([(edge * (-1) ** i, value) for i, value in enumerate(even)])
    cosines = [weighted([(inner * cosine[k][i], even[i]) for i in range(half + 1)]) for k in range(1, half)]
    sines = [weighted([(-inner * sine[k][i], odd[i]) for i in range(1, half)]) for k in range(1, half)]
    return [first, middle, *cosines, *sines]


def real_inverse(planes):
    count = len(planes)
    half = count // 2
    cosine, sine = angle_tables(count)
    edge, inner = 1 / math.sqrt(count), math.sqrt(2 / count)
    values = [None] * count
    for i in range(half + 1):
        even = weighted(
            [(edge, planes[0]), (edge * (-1) ** i, planes[1])]
            + [(inner * cosine[k][i], planes[k + 1]) for k in range(1, half)]
        )
        if i in (0, half):
            values[i] = even
            continue
        odd = weighted([(-inner * sine[k][i], planes[half + k]) for k in range(1, half)])
        values[i] = even + odd
        values[count - i] = even - odd
    return values


def halves_apart(count):
    order = [i // 2 + i % 2 * (count // 2) for i in range(count)]
    return order, [order.index(i) for i in range(count)]


def evens_first(count):
    order = [2 * i + odd for odd in range(2) for i in halves_apart(count // 2)[0]]
    return order, [order.index(i) for i in range(count)]


def plane_modes(count):
    half = count // 2
    return np.array([0, half, *range(1, half), *range(1, half)])


def tables(planes, lanes, blocks, length_x):
    half = blocks // 2
    t = np.arange(lanes)
    phases = np.arange(half)
    turn = 2 * np.pi * phases[:, None] * t[None, :] / length_x
    turns = np.concatenate([np.cos(turn), np.sin(turn)])
    product = 2 * np.pi * (t[:, None] * t[None, :] % lanes) / lanes
    scale = 1 / math.sqrt(lanes)
    c, s = np.cos(product) * scale, np.sin(product) * scale
    inner = np.block([[c, -s], [s, c]])
    root = math.sqrt(2.0)
    n = lanes // 2
    first = np.concatenate([c[:, :1], root * c[:, 1:n], c[:, n : n + 1], -root * s[:, 1:n]], axis=1)
    shifted = np.pi * (t[:, None] * (2 * np.arange(n)[None, :] + 1) % (2 * lanes)) / lanes
    middle = root * scale * np.concatenate([np.cos(shifted), -np.sin(shifted)], axis=1)
    outer = np.concatenate([first, middle], axis=1)
    mode_x = np.zeros((half, 2 * lanes))
    mode_x[1:] = phases[1:, None] + blocks * np.concatenate([t, t])[None, :]
    mode_x[0, : n + 1] = blocks * np.arange(n + 1)
    mode_x[0, n + 1 : lanes] = blocks * np.arange(1, n)
    mode_x[0, lanes:] = half + blocks * np.concatenate([np.arange(n), np.arange(n)])
    wave_x = (2 * np.sin(np.pi * mode_x / length_x)) ** 2
    wave_z = (2 * np.sin(np.pi * plane_modes(planes) / planes)) ** 2
    eigen_sum = grid_ratio * grid_ratio * (wave_z[:, None, None] + wave_x[None]) + shift_term
    decay = 2 * np.arcsinh(np.sqrt(eigen_sum) / 2)
    decay = decay.reshape(planes * half, 2 * lanes)
    turns = np.concatenate([turns[:half], turns[half:]], axis=1)
    matrices = np.concatenate([inner, outer])
    return jnp.asarray(matrices, jnp.float32), jnp.asarray(np.concatenate([decay, turns]), jnp.float32)


def split(values, count):
    parts = []
    for _ in range(count):
        parts.append(values.astype(jnp.bfloat16))
        values = values - parts[-1].astype(jnp.float32)
    return parts


def product(values, matrix, transposed=False):
    parts, matrix, rows = split(values, 3), split(matrix, 3), values.shape[0]
    dims = (((1,), (1 if transposed else 0,)), ((), ()))
    terms = []
    for j, piece in enumerate(matrix):
        stacked = parts[: len(parts) - j]
        stacked = jnp.concatenate(stacked) if len(stacked) > 1 else stacked[0]
        terms.append(lax.dot_general(stacked, piece, dims, preferred_element_type=jnp.float32))
    total = None
    for size in reversed(range(len(matrix))):
        for j in range(size + 1):
            i = size - j
            term = terms[j][i * rows : (i + 1) * rows]
            total = term if total is None else total + term
    return total


class Tables:
    def __init__(self, matrix_ref, ref, lanes, half):
        self.matrix_ref, self.ref, self.lanes, self.half = matrix_ref, ref, lanes, half

    def inner(self):
        return self.matrix_ref[: 2 * self.lanes, :]

    def outer(self, h):
        return self.matrix_ref[2 * self.lanes :, h * self.lanes : (h + 1) * self.lanes]

    def decay(self):
        return self.ref[: self.half, :]

    def turn(self, a):
        line = self.half + a
        return self.ref[line : line + 1, : self.lanes], self.ref[line : line + 1, self.lanes :]


def places(shape):
    return lax.broadcasted_iota(jnp.int32, shape, 0), lax.broadcasted_iota(jnp.int32, shape, 1)


def column_to_row(column, row, lane):
    return jnp.sum(jnp.where(row == lane, column, 0.0), axis=0, keepdims=True)


def row_to_column(line, row, lane):
    return jnp.sum(jnp.where(row == lane, line, 0.0), axis=1, keepdims=True)


def wall_keep(row, last_row, parts_y):
    is_wall = jnp.logical_and(row == last_row, lax.axis_index("gy") == parts_y - 1)
    return jnp.where(is_wall, 0.0, 1.0)


def source_kernel(
    planes,
    parts_y,
    stream_hbm,
    normal_hbm,
    span_hbm,
    table_hbm,
    matrix_hbm,
    out_ref,
    local_ref,
    matrix_ref,
    stream_ref,
    normal_ref,
    span_ref,
    done,
):
    half = local_ref.shape[0] // 2
    index = lax.axis_index("gx")
    chip, quarter = lax.div(index, 2), planes // 4
    plane_here = lax.rem(index, 2) * (planes // 2) + 2 * lax.rem(chip, quarter) + lax.div(chip, quarter)
    decay_rows = pl.ds(pl.multiple_of(plane_here * half, half), half)
    turn_rows = pl.ds(table_hbm.shape[0] - half, half)
    copies = [
        pltpu.make_async_copy(stream_hbm, stream_ref, done.at[0]),
        pltpu.make_async_copy(normal_hbm, normal_ref, done.at[1]),
        pltpu.make_async_copy(span_hbm, span_ref, done.at[2]),
        pltpu.make_async_copy(table_hbm.at[decay_rows, :], local_ref.at[:half, :], done.at[3]),
        pltpu.make_async_copy(table_hbm.at[turn_rows, :], local_ref.at[half:, :], done.at[4]),
        pltpu.make_async_copy(matrix_hbm, matrix_ref, done.at[5]),
    ]
    for copy in copies:
        copy.start()
    for copy in copies[:3]:
        copy.wait()
    cells = stream_ref.shape[1]
    rows = stream_ref.shape[0] // planes
    row, lane = places((rows, cells))
    keep = wall_keep(row, rows - 1, parts_y)

    def plane(ref, z):
        return ref[pl.ds(z, rows, stride=planes), :]

    main, rim = [], []
    span_before = plane(span_ref, planes - 1)
    for z in range(planes):
        stream, normal, span = plane(stream_ref, z), plane(normal_ref, z) * keep, plane(span_ref, z)
        stream_left = jnp.where(lane == 0, 0.0, pltpu.roll(stream, 1, 1))
        normal_turned = pltpu.roll(normal, 1, 0)
        normal_below = jnp.where(row == 0, 0.0, normal_turned)
        main.append(
            grid_ratio * (stream - stream_left) + (normal - normal_below) + grid_ratio * (span - span_before)
        )
        ends = column_to_row(stream[:, cells - 1 :], row, lane)
        rim.append(jnp.where(row == 0, -normal_turned, jnp.where(row == 1, -grid_ratio * ends, 0.0)))
        span_before = span
    main, rim = real_forward(main), real_forward(rim)
    for k in range(planes):
        put(out_ref, k, main[k], rim[k])
    for copy in copies[3:]:
        copy.wait()


def put(ref, index, main, rim):
    pairs = ref.shape[1] - 1
    for j in range(pairs):
        ref[index, j] = main[2 * j : 2 * j + 2, :]
    ref[index, pairs] = rim[:2, :]


def take(ref, held):
    count, pairs = ref.shape[0], ref.shape[1] - 1
    for i in range(count):
        for j in range(pairs):
            held[i, 2 * j : 2 * j + 2, :] = ref[i, j]
    return [held[i] for i in range(count)], [ref[i, pairs] for i in range(count)]


class Line:
    def __init__(self, decay, rows, parts_y):
        base = (lax.axis_index("gy") * rows).astype(jnp.float32)
        total = rows * parts_y
        self.step = jnp.exp(-decay)
        square, grown = self.step * self.step, jnp.exp(2.0 * decay)
        low = jnp.exp(-decay * (2.0 * base + 1.0))
        high = jnp.exp(-decay * (2.0 * (total - base) - 1.0))
        self.low, self.high = [], []
        for _ in range(rows + 1):
            self.low.append(1.0 + low)
            self.high.append(1.0 + high)
            low, high = low * square, high * grown
        self.decay, self.total = decay, total

    def gain(self):
        return -1.0 / ((jnp.exp(self.decay) - self.step) * (1.0 - jnp.exp(self.decay * (-2.0 * self.total))))


def modes_kernel(rows, parts_y, in_ref, matrix_ref, table_ref, send_ref, modes_ref, left, edge, held):
    blocks, _, _, lanes = in_ref.shape
    half = blocks // 2
    table = Tables(matrix_ref, table_ref, lanes, half)
    row, lane = places((rows, lanes))
    main, rim = take(in_ref, held)
    spot = evens_first(blocks)[1]
    main, rim = [main[spot[d]] for d in range(blocks)], [rim[spot[d]] for d in range(blocks)]
    for d in range(blocks):
        ends = row_to_column(rim[d - 1][1:2, :], row, lane)
        main[d] = main[d] + jnp.where(lane == 0, ends, 0.0)
    main = real_forward(main)
    rim = real_forward([piece[:1, :] for piece in rim])
    edge[...] = jnp.zeros_like(edge)
    left[...] = jnp.zeros_like(left)
    for h in range(2):
        edge[h, :rows, :] = main[h]
        edge[h, rows : rows + 1, :] = rim[h]
    for a in range(1, half):
        c, s = table.turn(a)
        for first, count, (re, im) in (
            (a, rows, (main[a + 1], main[half + a])),
            (rows * half + a, 1, (rim[a + 1], rim[half + a])),
        ):
            left[0, pl.ds(first, count, stride=half), :] = re * c + im * s
            left[1, pl.ds(first, count, stride=half), :] = im * c - re * s
    inner = product(jnp.concatenate([left[0], left[1]], axis=1), table.inner())
    for h in range(2):
        modes_ref[h, :, :] = inner[: (rows + 1) * half, h * lanes : (h + 1) * lanes]
        outer = product(edge[h], table.outer(h))
        modes_ref[h, pl.ds(0, rows, stride=half), :] = outer[:rows]
        modes_ref[h, rows * half : rows * half + 1, :] = outer[rows : rows + 1]
    spectrum = row_list(modes_ref, rows, half)
    line = Line(table.decay(), rows, parts_y)
    below = line.low[0] * spectrum[0]
    above = line.high[rows] * spectrum[rows]
    for i in range(1, rows + 1):
        below = line.low[i] * spectrum[i] + line.step * below
        above = line.high[rows - i] * spectrum[rows - i] + line.step * above
    for other in range(send_ref.shape[0]):
        send_ref[other, :half, :] = below
        send_ref[other, half:, :] = above


def row_list(modes_ref, rows, half):
    return [
        jnp.concatenate([modes_ref[h, i * half : (i + 1) * half, :] for h in range(2)], axis=1)
        for i in range(rows + 1)
    ]


def near_kernel(rows, near, in_ref, table_ref, mine_ref, send_ref):
    half = in_ref.shape[1] // 2
    step = jnp.exp(-rows * table_ref[:half, :])
    place, group = lax.rem(lax.axis_index("gy"), near), lax.div(lax.axis_index("gy"), near)
    below = above = jnp.zeros_like(step)
    spot = halves_apart(near)[1]
    for i in range(near):
        j = near - 1 - i
        mine_ref[:half, :] = jnp.where(place == i, below, mine_ref[:half, :]) if i else below
        mine_ref[half:, :] = jnp.where(place == j, above, mine_ref[half:, :]) if i else above
        below = in_ref[spot[i], :half, :] + step * below
        above = in_ref[spot[j], half:, :] + step * above
    for i, other in enumerate(halves_apart(send_ref.shape[0])[0]):
        send_ref[i, :, :] = jnp.where(group < other, below, above)


def entering(pieces_ref, mine, step):
    count = pieces_ref.shape[0]
    spot = halves_apart(count)[1]
    below = above = jnp.zeros_like(step)
    for i in range(count):
        j = count - 1 - i
        below = jnp.where(i < mine, pieces_ref[spot[i]] + step * below, below)
        above = jnp.where(j > mine, pieces_ref[spot[j]] + step * above, above)
    return below, above


def solve_kernel(rows, parts_y, near, in_ref, mine_ref, modes_ref, matrix_ref, table_ref, out_ref, left, edge):
    blocks, _, _, lanes = out_ref.shape
    half = blocks // 2
    table = Tables(matrix_ref, table_ref, lanes, half)
    row, lane = places((rows, lanes))
    decay = table.decay()
    place, group = lax.rem(lax.axis_index("gy"), near), lax.div(lax.axis_index("gy"), near)
    far_below, far_above = entering(in_ref, group, jnp.exp(-(rows * near) * decay))
    ahead = (rows * place).astype(jnp.float32)
    below = mine_ref[:half, :] + jnp.exp(-decay * ahead) * far_below
    above = mine_ref[half:, :] + jnp.exp(-decay * (rows * (near - 1) - ahead)) * far_above
    line = Line(decay, rows, parts_y)
    spectrum = row_list(modes_ref, rows, half)
    gain = line.gain()
    from_below = [line.low[0] * spectrum[0] + below]
    for i in range(1, rows + 1):
        from_below.append(line.low[i] * spectrum[i] + line.step * from_below[-1])
    from_above = above
    edge[...] = jnp.zeros_like(edge)
    for i in reversed(range(rows + 1)):
        solved = gain * (line.high[i] * from_below[i] + line.low[i] * from_above)
        for h, sign in ((0, 1.0), (1, -1.0)):
            part = solved[:, h * lanes : (h + 1) * lanes]
            edge[h, i : i + 1, :] = part[:1, :]
            left[h, i * half : (i + 1) * half, :] = sign * part
        from_above = line.step * (from_above + line.high[i] * spectrum[i])
    left[:, (rows + 1) * half :, :] = jnp.zeros_like(left[:, (rows + 1) * half :, :])
    inner = product(jnp.concatenate([left[0], left[1]], axis=1), table.inner())
    main, rim = [], []
    for h in range(2):
        left[h, :, :] = inner[:, h * lanes : (h + 1) * lanes]
        outer = product(edge[h], table.outer(h), transposed=True)
        main.append(outer[:rows])
        rim.append(outer[rows : rows + 1])
    main, rim = main + [None] * (blocks - 2), rim + [None] * (blocks - 2)
    for a in range(1, half):
        c, s = table.turn(a)
        for planes, first, count in ((main, a, rows), (rim, rows * half + a, 1)):
            re = left[0, pl.ds(first, count, stride=half), :]
            im = left[1, pl.ds(first, count, stride=half), :]
            planes[a + 1] = re * c + im * s
            planes[half + a] = re * s - im * c
    main, rim = real_inverse(main), real_inverse(rim)
    spot = evens_first(blocks)[1]
    for d in range(blocks):
        ends = column_to_row(main[(d + 1) % blocks][:, :1], row, lane)
        put(out_ref, spot[d], main[d], jnp.where(row == 0, rim[d], ends))


def correct_kernel(
    parts_y, in_ref, stream_ref, normal_ref, span_ref, pressure_ref, stream_out, normal_out, span_out, held
):
    planes, _, _, cells = in_ref.shape
    rows = stream_ref.shape[0] // planes
    row, lane = places((rows, cells))
    keep = wall_keep(row, rows - 1, parts_y)
    pressure, rim = take(in_ref, held)
    pressure, rim = real_inverse(pressure), real_inverse(rim)
    for z in range(planes):
        here = pl.ds(z, rows, stride=planes)
        p = pressure[z]
        upper = jnp.where(row == rows - 1, rim[z][:1, :], pltpu.roll(p, rows - 1, 0))
        right = jnp.where(lane == cells - 1, row_to_column(rim[z][1:2, :], row, lane), pltpu.roll(p, cells - 1, 1))
        pressure_ref[here, :] = p
        stream_out[here, :] = stream_ref[here, :] - grid_ratio * (right - p)
        normal_out[here, :] = (normal_ref[here, :] - (upper - p)) * keep
        span_out[here, :] = span_ref[here, :] - grid_ratio * (pressure[(z + 1) % planes] - p)


def shape_of(*dims):
    return jax.ShapeDtypeStruct(dims, jnp.float32)


def per_device(stream_vel, normal_vel, span_vel):
    rows, planes, cells = stream_vel.shape
    parts_x, parts_y = lax.axis_size("gx"), lax.axis_size("gy")
    blocks, half = parts_x, parts_x // 2
    near = 1 << (parts_y.bit_length() // 2)
    far = parts_y // near
    if planes != parts_x or rows != half or near * far != parts_y:
        raise ValueError("unsupported sizes")
    matrices, table = tables(planes, cells, blocks, cells * parts_x)
    near_groups = [[i * near + k for k in halves_apart(near)[0]] for i in range(far)]
    far_groups = [[i + k * near for k in halves_apart(far)[0]] for i in range(near)]
    flat = [a.reshape(rows * planes, cells) for a in (stream_vel, normal_vel, span_vel)]
    message = shape_of(blocks, rows // 2 + 1, 2, cells)
    held = pltpu.VMEM((blocks, rows, cells), jnp.float32)
    room = pltpu.CompilerParams(vmem_limit_bytes=8 << 20)
    scratch = [
        pltpu.VMEM((2, (rows + 2) * half, cells), jnp.float32),
        pltpu.VMEM((2, 2 * rows, cells), jnp.float32),
    ]

    kept = [matrices, *flat]
    sent, local, *kept = pl.pallas_call(
        functools.partial(source_kernel, planes, parts_y),
        out_shape=(message, shape_of(2 * half, 2 * cells), *(jax.ShapeDtypeStruct(a.shape, a.dtype) for a in kept)),
        in_specs=[pl.BlockSpec(memory_space=pltpu.HBM)] * 5,
        scratch_shapes=[pltpu.SemaphoreType.DMA((6,))],
        compiler_params=room,
        name="source",
    )(*(pltpu.with_memory_space_constraint(a, pltpu.HBM) for a in (*flat, table, matrices)))
    matrices, *flat = kept
    taken = lax.all_to_all(sent, "gx", 0, 0, axis_index_groups=[evens_first(blocks)[0]])
    sent, modes = pl.pallas_call(
        functools.partial(modes_kernel, rows, parts_y),
        out_shape=(shape_of(near, 2 * half, 2 * cells), shape_of(2, (rows + 1) * half, cells)),
        scratch_shapes=[*scratch, held],
        compiler_params=room,
        name="modes",
    )(taken, matrices, local)
    taken = lax.all_to_all(sent, "gy", 0, 0, axis_index_groups=near_groups)
    mine, sent = pl.pallas_call(
        functools.partial(near_kernel, rows, near),
        out_shape=(shape_of(2 * half, 2 * cells), shape_of(far, half, 2 * cells)),
        compiler_params=room,
        name="near",
    )(taken, local)
    taken = lax.all_to_all(sent, "gy", 0, 0, axis_index_groups=far_groups)
    sent = pl.pallas_call(
        functools.partial(solve_kernel, rows, parts_y, near),
        out_shape=message,
        scratch_shapes=scratch,
        compiler_params=room,
        name="solve",
    )(taken, mine, modes, matrices, local)
    taken = lax.all_to_all(sent, "gx", 0, 0, axis_index_groups=[evens_first(blocks)[0]])
    outs = pl.pallas_call(
        functools.partial(correct_kernel, parts_y),
        out_shape=(shape_of(rows * planes, cells),) * 4,
        scratch_shapes=[held],
        compiler_params=room,
        name="correct",
    )(taken, *flat)
    return tuple(a.reshape(rows, planes, cells) for a in outs)


def solution(mesh):
    spec = P("gy", None, "gx")
    return jax.shard_map(
        per_device, mesh=mesh, in_specs=(spec,) * 3, out_specs=(spec,) * 4, check_vma=False
    )
```
